32 devices in a mesh: leaf: 8 (over z, y), col: 4 (over x, core).
Axes of the slice: x: 2, y: 2, z: 4, core: 2. Of those that a mesh axis runs over, the one named last changes fastest.
Arguments:
- leaf_rhs: float32 [7168, 512], P('leaf', 'col'), may hold values from -6 to 6
- leaf_inverse: float32 [56, 128, 128], P('leaf'), may hold values from -0.5 to 0.5
- leaf_blocks: float32 [168, 128, 128], P('leaf'), may hold values from -0.1875 to 0.1875
- leaf_pattern: int32 [8, 21], P('leaf'), may hold values 0 or 1
- leaf_coupling: float32 [2048, 512], P('leaf'), may hold values from -0.0625 to 0.0625
- sep_rhs: float32 [1536, 512], P('leaf', 'col'), may hold values from -6 to 6
- sep_inverse: float32 [1536, 512], P('leaf', 'col'), may hold values from -0.25 to 0.25
- sep_coupling: float32 [1024, 512], P('leaf', 'col'), may hold values from -0.09375 to 0.09375
Outputs:
- leaf_solution: float32 [7168, 512], P('leaf', 'col')
- sep_solution: float32 [1536, 512], P('leaf', 'col')
The draws below stay inside these ranges and needn't reach their ends.
Inputs may be any that keep to these rules, and one draw needn't show every extreme that they name: `leaf_pattern`: 1 where a factor block below the diagonal is nonzero, 0 where it is zero.
All inputs are finite; a program needn't handle non-finite values.
Results may differ from the reference program's by a relative error of at most 0.00011.
Values sent between devices are 32-bit elements; how exact they have to be, the bound alone decides.
A program may use at most 64 MiB of HBM per device.

```python
import jax
import jax.numpy as jnp
from jax import lax

BLK = 128
NB = 7
SEP = 512
NRHS = 512
LR = 896
NPAIR = 21
LEVELS = 2
SR = 192
VC = 128
N_LEAF = 8


def plant(entries, own_key, low, top_value):
    longest = entries.shape.index(max(entries.shape))
    spots = []
    for shift in (0, 1):
        where = [jax.random.randint(jax.random.fold_in(own_key, axis), (), 0, length) for axis, length in enumerate(entries.shape)]
        where[longest] = (where[longest] + shift) % entries.shape[longest]
        spots.append(tuple(where))
    return entries.at[spots[0]].set(low).at[spots[1]].set(top_value)


def shard_levels(key, shape, pieces, least, largest):
    level = 1.0
    for position, blocks in pieces:
        draws = jax.random.uniform(jax.random.fold_in(jax.random.fold_in(key, 6), position), (blocks,), jnp.float32, least / len(pieces), largest / len(pieces))
        level = level * jnp.repeat(jnp.exp(draws), shape[position] // blocks).reshape((-1,) + (1,) * (len(shape) - 1 - position))
    return level


def gaussian(own_key, dims, scale, most, cuts=(), kind=jnp.bfloat16):
    values = scale * jax.random.normal(own_key, dims, jnp.float32)
    if cuts:
        values = values * shard_levels(own_key, dims, cuts, -0.22, 0.18)
    return jnp.clip(values, -most, most).astype(kind)


def setup_inputs(seed: int = 0) -> dict:
    seeds = jax.random.split(jax.random.key(seed), 9)
    leaf_rhs = gaussian(seeds[0], (N_LEAF * LR, NRHS), 1.0, 6.0, ((0, 8), (1, 4)), jnp.float32)
    leaf_inverse = gaussian(seeds[1], (N_LEAF * NB, BLK, BLK), BLK ** -0.5, 0.5, ((0, 8),), jnp.float32)
    leaf_blocks = gaussian(seeds[2], (N_LEAF * NPAIR, BLK, BLK), (BLK * NB) ** -0.5, 0.1875, ((0, 8),), jnp.float32)
    leaf_pattern = plant((jax.random.randint(seeds[3], (N_LEAF, NPAIR), 0, 2) < 1).astype(jnp.int32), jax.random.fold_in(seeds[3], 1), 0, 1)
    leaf_coupling = gaussian(seeds[4], (N_LEAF * LEVELS * BLK, SEP), (64 * BLK) ** -0.5, 0.0625, ((0, 8),), jnp.float32)
    sep_rhs = gaussian(seeds[5], (N_LEAF * SR, NRHS), 1.0, 6.0, ((0, 8), (1, 4)), jnp.float32)
    sep_inverse = gaussian(seeds[6], (N_LEAF * SR, SEP), SEP ** -0.5, 0.25, ((0, 8), (1, 4)), jnp.float32)
    sep_coupling = gaussian(seeds[7], (N_LEAF * VC, SEP), (8 * SEP) ** -0.5, 0.09375, ((0, 8), (1, 4)), jnp.float32)
    return {"leaf_rhs": leaf_rhs, "leaf_inverse": leaf_inverse, "leaf_blocks": leaf_blocks, "leaf_pattern": leaf_pattern, "leaf_coupling": leaf_coupling, "sep_rhs": sep_rhs, "sep_inverse": sep_inverse, "sep_coupling": sep_coupling}


HIGH = lax.Precision.HIGHEST


def group_sizes(leaf_count):
    result = []
    for level_index in range(1, 5):
        group_span = 4 ** level_index
        if group_span // 4 < leaf_count:
            result.append(min(group_span, leaf_count))
    return result


def grouped(piece, group_size, leaf_count):
    return piece.reshape(leaf_count // group_size, group_size * piece.shape[1], piece.shape[2])


def reference(leaf_rhs, leaf_inverse, leaf_blocks, leaf_pattern, leaf_coupling, sep_rhs, sep_inverse, sep_coupling):
    leaf_count = N_LEAF
    block_count = NB
    block_rows = BLK
    sep_rows = SEP
    columns = NRHS
    rhs_blocks = leaf_rhs.reshape(leaf_count, block_count, block_rows, columns)
    inverse = leaf_inverse.reshape(leaf_count, block_count, block_rows, block_rows)
    weighted = leaf_blocks.reshape(leaf_count, -1, block_rows, block_rows) * leaf_pattern.astype(jnp.float32)[:, :, None, None]
    column_starts = []
    running = 0
    for column_index in range(block_count):
        column_starts.append(running)
        running = running + block_count - 1 - column_index
    pending = [rhs_blocks[:, i] for i in range(block_count)]
    forward = []
    for column_index in range(block_count):
        solved = jnp.einsum('nab,nbc->nac', inverse[:, column_index], pending[column_index], precision=HIGH)
        forward.append(solved)
        for later_index in range(column_index + 1, block_count):
            pair_index = column_starts[column_index] + later_index - column_index - 1
            pending[later_index] = pending[later_index] - jnp.einsum('nab,nbc->nac', weighted[:, pair_index], solved, precision=HIGH)
    sizes_list = group_sizes(leaf_count)
    level_total = len(sizes_list)
    row_counts = [sep_rows // size_item for size_item in sizes_list]
    offsets = []
    running = 0
    for row_count in row_counts:
        offsets.append(running)
        running = running + row_count
    sep_right = sep_rhs.reshape(leaf_count, -1, columns)
    sep_inv = sep_inverse.reshape(leaf_count, -1, sep_rows)
    sep_cpl = sep_coupling.reshape(leaf_count, -1, sep_rows)
    couple = leaf_coupling.reshape(leaf_count, level_total, block_rows, sep_rows)
    last_block = forward[-1]
    forward_levels = []
    for level_index in range(level_total):
        group_size = sizes_list[level_index]
        row_count = row_counts[level_index]
        row_offset = offsets[level_index]
        leaf_term = jnp.einsum('nks,nkc->nsc', couple[:, level_index], last_block, precision=HIGH)
        leaf_term = leaf_term.reshape(leaf_count // group_size, group_size, sep_rows, columns).sum(1)
        summed = grouped(sep_right[:, row_offset:row_offset + row_count], group_size, leaf_count) - leaf_term
        if level_index > 0:
            child_size = sizes_list[level_index - 1]
            child_count = row_counts[level_index - 1]
            child_offset = offsets[level_index - 1]
            child_matrix = grouped(sep_cpl[:, child_offset:child_offset + child_count], child_size, leaf_count)
            child_term = jnp.einsum('nrs,nrc->nsc', child_matrix, forward_levels[-1], precision=HIGH)
            summed = summed - child_term.reshape(leaf_count // group_size, group_size // child_size, sep_rows, columns).sum(1)
        diag_matrix = grouped(sep_inv[:, row_offset:row_offset + row_count], group_size, leaf_count)
        forward_levels.append(jnp.einsum('nsr,nrc->nsc', diag_matrix, summed, precision=HIGH))
    back_levels = [None] * level_total
    for level_index in reversed(range(level_total)):
        group_size = sizes_list[level_index]
        row_count = row_counts[level_index]
        row_offset = offsets[level_index]
        target = forward_levels[level_index]
        if level_index < level_total - 1:
            parent_size = sizes_list[level_index + 1]
            child_matrix = grouped(sep_cpl[:, row_offset:row_offset + row_count], group_size, leaf_count)
            parent_rep = jnp.repeat(back_levels[level_index + 1], parent_size // group_size, axis=0)
            target = target - jnp.einsum('nrs,nsc->nrc', child_matrix, parent_rep, precision=HIGH)
        diag_matrix = grouped(sep_inv[:, row_offset:row_offset + row_count], group_size, leaf_count)
        back_levels[level_index] = jnp.einsum('nsr,nsc->nrc', diag_matrix, target, precision=HIGH)
    correction = jnp.zeros((leaf_count, block_rows, columns), jnp.float32)
    for level_index in range(level_total):
        spread = jnp.repeat(back_levels[level_index], sizes_list[level_index], axis=0)
        correction = correction + jnp.einsum('nks,nsc->nkc', couple[:, level_index], spread, precision=HIGH)
    pending = list(forward)
    pending[-1] = pending[-1] - correction
    backward = [None] * block_count
    for column_index in reversed(range(block_count)):
        target = pending[column_index]
        for later_index in range(column_index + 1, block_count):
            pair_index = column_starts[column_index] + later_index - column_index - 1
            target = target - jnp.einsum('nab,nac->nbc', weighted[:, pair_index], backward[later_index], precision=HIGH)
        backward[column_index] = jnp.einsum('nab,nac->nbc', inverse[:, column_index], target, precision=HIGH)
    leaf_solution = jnp.stack(backward, axis=1).reshape(leaf_count * block_count * block_rows, columns)
    sep_pieces = [back_levels[i].reshape(leaf_count, row_counts[i], columns) for i in range(level_total)]
    sep_solution = jnp.concatenate(sep_pieces, axis=1).reshape(-1, columns)
    return leaf_solution, sep_solution
```

```python
import functools

import jax
import jax.numpy as jnp
from jax import lax
from jax.experimental import pallas as pl
from jax.experimental.pallas import tpu as pltpu
from jax.sharding import PartitionSpec as P

HIGH = lax.Precision.HIGHEST
F32 = jnp.float32
BF16 = jnp.bfloat16
NN = ((1,), (0,))
NT = ((1,), (1,))


def from_partner(shard, axis, apart):
    return lax.ppermute(shard, axis, [(i, i ^ 1 << apart) for i in range(lax.axis_size(axis))])


def product(left_side, right_side):
    return jnp.dot(left_side, right_side, precision=HIGH, preferred_element_type=jnp.float32)


def product_first(left_side, right_side):
    return lax.dot_general(
        left_side,
        right_side,
        (((0,), (0,)), ((), ())),
        precision=HIGH,
        preferred_element_type=jnp.float32,
    )


def group_sizes(leaf_count):
    result = []
    for level_index in range(1, 5):
        group_span = 4**level_index
        if group_span // 4 < leaf_count:
            result.append(min(group_span, leaf_count))
    return result


def group_total(partial_value, group_size):
    bit_count = group_size.bit_length() - 1
    for bit_place in range(bit_count):
        partial_value = partial_value + from_partner(partial_value, "leaf", bit_place)
    return partial_value


def shards(
    leaf_rhs,
    leaf_inverse,
    leaf_blocks,
    leaf_pattern,
    leaf_coupling,
    sep_rhs,
    sep_inverse,
    sep_coupling,
):
    inverse_full, coupling_full = (
        lax.all_gather(sep_inverse, "col", axis=1, tiled=True),
        lax.all_gather(sep_coupling, "col", axis=1, tiled=True),
    )
    leaf_count = lax.axis_size("leaf")
    position = lax.axis_index("leaf")
    block_count = leaf_inverse.shape[0]
    block_rows = leaf_inverse.shape[1]
    columns = leaf_rhs.shape[1]
    sep_rows = inverse_full.shape[1]
    weighted = leaf_blocks * leaf_pattern[0].astype(jnp.float32)[:, None, None]
    rhs_blocks = leaf_rhs.reshape(block_count, block_rows, columns)
    column_starts = []
    running = 0
    for column_index in range(block_count):
        column_starts.append(running)
        running = running + block_count - 1 - column_index
    pending = [rhs_blocks[i] for i in range(block_count)]
    forward = []
    for column_index in range(block_count):
        solved = product(leaf_inverse[column_index], pending[column_index])
        forward.append(solved)
        below_count = block_count - 1 - column_index
        if below_count:
            pair_start = column_starts[column_index]
            column_blocks = weighted[pair_start : pair_start + below_count].reshape(
                below_count * block_rows, block_rows
            )
            update = product(column_blocks, solved).reshape(below_count, block_rows, columns)
            for later_index in range(below_count):
                pending[column_index + 1 + later_index] = (
                    pending[column_index + 1 + later_index] - update[later_index]
                )
    sizes_list = group_sizes(leaf_count)
    level_total = len(sizes_list)
    row_counts = [sep_rows // size_item for size_item in sizes_list]
    offsets = []
    running = 0
    for row_count in row_counts:
        offsets.append(running)
        running = running + row_count
    last_block = forward[-1]
    level_pieces = []
    for level_index in range(level_total):
        group_size = sizes_list[level_index]
        row_count = row_counts[level_index]
        row_offset = offsets[level_index]
        row_start = position % group_size * row_count
        coupling_rows = leaf_coupling[level_index * block_rows : (level_index + 1) * block_rows]
        partial_value = -product_first(coupling_rows, last_block)
        if level_index > 0:
            child_offset = offsets[level_index - 1]
            child_count = row_counts[level_index - 1]
            partial_value = partial_value - product_first(
                coupling_full[child_offset : child_offset + child_count], level_pieces[-1]
            )
        own_rows = (
            lax.dynamic_slice_in_dim(partial_value, row_start, row_count, 0)
            + sep_rhs[row_offset : row_offset + row_count]
        )
        partial_value = lax.dynamic_update_slice_in_dim(partial_value, own_rows, row_start, 0)
        summed = group_total(partial_value, group_size)
        level_pieces.append(product(inverse_full[row_offset : row_offset + row_count], summed))
    correction = jnp.zeros((block_rows, columns), jnp.float32)
    solution_pieces = [None] * level_total
    parent_full = None
    for level_index in reversed(range(level_total)):
        group_size = sizes_list[level_index]
        row_count = row_counts[level_index]
        row_offset = offsets[level_index]
        row_start = position % group_size * row_count
        target = level_pieces[level_index]
        if parent_full is not None:
            target = target - product(
                coupling_full[row_offset : row_offset + row_count], parent_full
            )
        partial_value = product_first(inverse_full[row_offset : row_offset + row_count], target)
        parent_full = group_total(partial_value, group_size)
        solution_pieces[level_index] = lax.dynamic_slice_in_dim(
            parent_full, row_start, row_count, 0
        )
        correction = correction + product(
            leaf_coupling[level_index * block_rows : (level_index + 1) * block_rows], parent_full
        )
    pending = list(forward)
    pending[-1] = pending[-1] - correction
    backward = [None] * block_count
    for column_index in reversed(range(block_count)):
        target = pending[column_index]
        below_count = block_count - 1 - column_index
        if below_count:
            pair_start = column_starts[column_index]
            column_blocks = weighted[pair_start : pair_start + below_count].reshape(
                below_count * block_rows, block_rows
            )
            later_blocks = jnp.concatenate(backward[column_index + 1 :], 0)
            target = target - product_first(column_blocks, later_blocks)
        backward[column_index] = product_first(leaf_inverse[column_index], target)
    return (jnp.concatenate(backward, 0), jnp.concatenate(solution_pieces, 0))


def halves(value):
    top = value.astype(BF16)
    return top, (value - top.astype(F32)).astype(BF16)


def mm(left_side, right_side, dims=NN):
    return lax.dot_general(
        left_side, right_side, (dims, ((), ())), preferred_element_type=F32
    )


def wide(left_top, left_low, right_both):
    n = right_both.shape[1] // 2
    both = mm(left_top, right_both)
    return both[:, :n] + both[:, n:] + mm(left_low, right_both[:, :n])


def tall(left_side, right_top, right_low, dims=NN):
    n = left_side.shape[0]
    top, low = halves(left_side)
    both = mm(jnp.concatenate([top, low], 0), right_top, dims)
    return both[:n] + both[n:] + mm(top, right_low, dims)


def whole_kernel(
    rhs_far, inv_far, blk_far, pat_far, cpl_far, srhs_far, sinv, scpl,
    solved, lifted, fixed, sout,
    rhs, inv, blk, pat, cpl, srhs,
    l_top, l_low, xt_top, xt_low,
    e_top, e_low, d1b, cb, d2b, d1_top, d1_low, c_top, c_low, d2_top, d2_low,
    pad, part, ra, acc, rb, tsend, trecv, xg, tmp, send, recv, near,
):
    leaf = lax.axis_index("leaf")
    col = lax.axis_index("col")
    y = lax.rem(leaf, 2)
    z0 = lax.rem(lax.div(leaf, 2), 2)
    z1 = lax.div(leaf, 4)
    core = lax.rem(col, 2)
    x = lax.div(col, 2)
    to_core = (leaf, col + 1 - 2 * core)
    to_x = (leaf, col + 2 - 4 * x)
    to_y = (leaf + 1 - 2 * y, col)
    to_z0 = (leaf + 2 - 4 * z0, col)
    to_z1 = (leaf + 4 - 8 * z1, col)

    barrier = pltpu.get_barrier_semaphore()
    partners = (to_core, to_x, to_y, to_z0, to_z1)
    for partner in partners:
        pl.semaphore_signal(
            barrier, inc=1, device_id=partner, device_id_type=pl.DeviceIdType.MESH
        )
    nb, br = inv.shape[0], inv.shape[1]
    n = rhs.shape[1]
    sep = cpl.shape[1]
    half = sep // 2
    r1, r2 = sep // 4, sep // 8
    w = n // 4
    starts = []
    running = 0
    for j in range(nb):
        starts.append(running)
        running += nb - 1 - j

    loads = []

    def fetch(src, dst):
        copy = pltpu.make_async_copy(src, dst, near.at[len(loads)])
        loads.append(copy)
        copy.start()
        return copy

    own = [
        fetch(sinv.at[pl.ds(0, r1)], d1b.at[z0, y, x, core]),
        fetch(scpl, cb.at[z0, y, x, core]),
        fetch(sinv.at[pl.ds(r1, r2)], d2b.at[z1, z0, y, x, core]),
    ]
    got_pat = fetch(pat_far, pat)
    got_inv = fetch(inv_far, inv)
    got_rhs = fetch(rhs_far, rhs)
    got_blk = []
    for j in range(nb - 1):
        box = pl.ds(starts[j], nb - 1 - j)
        got_blk.append(fetch(blk_far.at[box], blk.at[box]))
    got_cpl = fetch(cpl_far, cpl)
    got_srhs = fetch(srhs_far, srhs)


    copies = []

    def ship(src, dst, target):
        i = len(copies)
        copy = pltpu.make_async_remote_copy(
            src_ref=src, dst_ref=dst, send_sem=send.at[i], recv_sem=recv.at[i],
            device_id=target, device_id_type=pl.DeviceIdType.MESH,
        )
        copies.append(copy)
        copy.start()
        return copy

    got_pat.wait()
    got_inv.wait()
    got_rhs.wait()

    def at(i):
        return slice(i * br, (i + 1) * br)

    def load_column(j):
        if j < nb - 1:
            got_blk[j].wait()
        l_top[at(j), at(j)], l_low[at(j), at(j)] = halves(inv[j])
        for i in range(j + 1, nb):
            p = starts[j] + i - j - 1
            block = blk[p] * pat[0, p].astype(F32)
            l_top[at(i), at(j)], l_low[at(i), at(j)] = halves(block)

    pending = [rhs[at(i)] for i in range(nb)]
    forward = [None] * nb

    def forward_step(j):
        load_column(j)
        top, low = halves(pending[j])
        solved_j = wide(l_top[at(j), at(j)], l_low[at(j), at(j)], jnp.concatenate([top, low], 1))
        forward[j] = solved_j
        top, low = halves(solved_j)
        both = jnp.concatenate([top, low], 1)
        for i in range(j + 1, nb):
            pending[i] = pending[i] - wide(l_top[at(i), at(j)], l_low[at(i), at(j)], both)

    for j in range(nb):
        forward_step(j)
    got_cpl.wait()
    e_top[...], e_low[...] = halves(cpl[...])

    got_srhs.wait()
    last_t = forward[nb - 1].T

    def make_part(l):
        pad[...] = jnp.zeros_like(pad)
        if l == 0:
            pad[pl.ds(pl.multiple_of((2 * z0 + y) * r1, r1), r1), :] = srhs[0:r1]
        else:
            pad[pl.ds(pl.multiple_of(leaf * r2, r2), r2), :] = srhs[r1 : r1 + r2]
        term = pad[...].T - tall(last_t, e_top[at(l), :], e_low[at(l), :])
        for h in range(2):
            part[l, h] = term[:, h * half : (h + 1) * half].reshape(2, 2, w, half)

    def send_part(l):
        return (
            ship(part.at[l, 0, :, 1 - y], ra.at[l, 0], to_y),
            ship(part.at[l, 1, 1 - z0, :], ra.at[l, 1], to_z0),
        )

    make_part(0)
    make_part(1)
    for copy in own:
        copy.wait()
    pl.semaphore_wait(barrier, len(partners))

    orders = ("xyz", "yzx", "zxy")
    partner_of = {"x": to_x, "y": to_y, "z": to_z0}

    def row_parts(count):
        units = count // 8
        first = (units + 2) // 3
        second = (units - first + 1) // 2
        sizes = (first * 8, second * 8, count - 8 * (first + second))
        return ((0, sizes[0]), (sizes[0], sizes[1]), (sizes[0] + sizes[1], sizes[2]))

    def stage(ref, step, source=None, lead=()):
        sent = []
        for order, (begin, size) in zip(orders, row_parts(ref.shape[-2])):
            have = order[:step]
            where = lead + tuple(
                slice(None) if name in have else place
                for name, place in (("z", z0), ("y", y), ("x", x))
            ) + (core, pl.ds(begin, size))
            box = ref.at[where]
            src = box if source is None else source.at[pl.ds(begin, size)]
            sent.append(ship(src, box, partner_of[order[step]]))
        return sent

    def arrived(sent):
        for copy in sent:
            copy.wait_recv()

    every = (slice(None),)
    d1_a = stage(d1b, 0, sinv)
    a1 = send_part(0)
    c_a = stage(cb, 0, scpl)
    d2_z = ship(sinv.at[pl.ds(r1, r2)], d2b.at[z1, z0, y, x, core], to_z1)

    def second(l, pair):
        pair[0].wait_recv()
        acc[l, 0] = part[l, 0, :, y] + ra[l, 0]
        first = ship(acc.at[l, 0, 1 - z0], rb.at[l, 0], to_z0)
        pair[1].wait_recv()
        acc[l, 1] = part[l, 1, z0] + ra[l, 1]
        return first, ship(acc.at[l, 1, 1 - y], rb.at[l, 1], to_y)

    def total(l, pair):
        pair[0].wait_recv()
        pair[1].wait_recv()
        return jnp.concatenate([acc[l, 0, z0] + rb[l, 0], acc[l, 1, y] + rb[l, 1]], 1)

    row = lax.broadcasted_iota(jnp.int32, (br, br), 0)
    column = lax.broadcasted_iota(jnp.int32, (br, br), 1)
    unit = jnp.where(row == column, 1.0, 0.0).astype(F32)

    def backward_step(i):
        first = forward[i].T
        below = unit if i == nb - 1 else jnp.zeros((br, br), F32)
        target = jnp.concatenate([first, below], 0)
        if i < nb - 1:
            rest = slice((i + 1) * br, nb * br)
            target = target - (
                mm(xt_top[:, rest], l_top[rest, at(i)])
                + mm(xt_low[:, rest], l_top[rest, at(i)])
                + mm(xt_top[:, rest], l_low[rest, at(i)])
            )
        value = tall(target, l_top[at(i), at(i)], l_low[at(i), at(i)])
        xt_top[:, at(i)], xt_low[:, at(i)] = halves(value)
        solved[at(i), :] = value[:n].T
        top, low = halves(value[n:].T)
        lifted[at(i), 0:br] = top
        lifted[at(i), br : 2 * br] = low

    def spread(src, top_ref, low_ref, rows, lead):
        for k in range(lead):
            for c in range(4):
                if lead == 4:
                    tile = src[k // 2, k % 2, c // 2, c % 2]
                else:
                    tile = src[k // 4, k // 2 % 2, k % 2, c // 2, c % 2]
                where = (slice(k * rows, (k + 1) * rows), slice(c * tile.shape[1], (c + 1) * tile.shape[1]))
                top, low = halves(tile)
                top_ref[where] = top
                low_ref[where] = low

    arrived(d1_a)
    d1_b = stage(d1b, 1)
    b1 = second(0, a1)
    arrived(c_a)
    c_b = stage(cb, 1)
    arrived(d1_b)
    d1_c = stage(d1b, 2)
    a2 = send_part(1)
    arrived(c_b)
    c_c = stage(cb, 2)
    d2_z.wait_recv()
    d2_a = stage(d2b, 0, lead=every)
    s_1 = total(0, b1)
    b2 = second(1, a2)
    arrived(d1_c)
    d1_d = ship(d1b.at[:, :, :, core], d1b.at[:, :, :, core], to_core)
    backward_step(6)
    arrived(d2_a)
    d2_b = stage(d2b, 1, lead=every)
    d1_d.wait_recv()
    spread(d1b, d1_top, d1_low, r1, 4)
    z_1 = tall(s_1, d1_top[...], d1_low[...], NT)
    arrived(c_c)
    c_d = ship(cb.at[:, :, :, core], cb.at[:, :, :, core], to_core)
    s_2 = total(1, b2)
    c_d.wait_recv()
    spread(cb, c_top, c_low, r1, 4)
    tsend[...] = s_2 - tall(z_1, c_top[...], c_low[...])
    ts = ship(tsend, trecv, to_z1)
    arrived(d2_b)
    d2_c = stage(d2b, 2, lead=every)
    backward_step(5)
    backward_step(4)
    arrived(d2_c)
    d2_d = ship(d2b.at[:, :, :, :, core], d2b.at[:, :, :, :, core], to_core)
    backward_step(3)
    backward_step(2)
    d2_d.wait_recv()
    spread(d2b, d2_top, d2_low, r2, 8)
    ts.wait_recv()
    z_2 = tall(tsend[...] + trecv[...], d2_top[...], d2_low[...], NT)
    x_2 = tall(z_2, d2_top[...], d2_low[...])

    def give(l, value):
        xg[l, 0, z0, y] = value[:, :half]
        xg[l, 1, z0, y] = value[:, half:]
        return (
            ship(xg.at[l, 0, z0, y], xg.at[l, 0, z0, y], to_y),
            ship(xg.at[l, 1, z0, y], xg.at[l, 1, z0, y], to_z0),
        )

    def give_more(l, pair):
        pair[0].wait_recv()
        first = ship(xg.at[l, 0, z0], xg.at[l, 0, z0], to_z0)
        pair[1].wait_recv()
        return first, ship(xg.at[l, 1, :, y], xg.at[l, 1, :, y], to_y)

    def correction(l, pair):
        result = None
        for h in range(2):
            pair[h].wait_recv()
            top, low = halves(xg[l, h].reshape(n, half))
            lanes = slice(h * half, (h + 1) * half)
            e_t, e_l = e_top[at(l), lanes], e_low[at(l), lanes]
            term = mm(e_t, top, NT) + mm(e_t, low, NT) + mm(e_l, top, NT)
            result = term if result is None else result + term
        return result

    a2 = give(1, x_2)
    x_1 = tall(z_1 - tall(x_2, c_top[...], c_low[...], NT), d1_top[...], d1_low[...])
    a1 = give(0, x_1)
    a2 = give_more(1, a2)
    backward_step(1)
    a1 = give_more(0, a1)
    backward_step(0)
    fix = correction(1, a2)
    tmp[...] = xg[1, z1, :, :, :, pl.ds(pl.multiple_of(z0 * 2 * r2, 2 * r2), 2 * r2)].reshape(n, 2 * r2).T
    sout[r1 : r1 + r2, :] = tmp[pl.ds(pl.multiple_of(y * r2, r2), r2), :]
    fix = fix + correction(0, a1)
    top, low = halves(fix)
    fixed[...] = jnp.concatenate([top, low], 1)
    sout[0:r1, :] = xg[0, z0, :, :, :, pl.ds(pl.multiple_of(y * r1, r1), r1)].reshape(n, r1).T
    for copy in copies:
        copy.wait_send()


def fused(leaf_rhs, leaf_inverse, leaf_blocks, leaf_pattern, leaf_coupling, sep_rhs, sep_inverse, sep_coupling):
    rows, n = leaf_rhs.shape
    br = leaf_inverse.shape[1]
    sep = leaf_coupling.shape[1]
    half, w = sep // 2, n // 4
    r1, r2 = sep // 4, sep // 8
    tile = sep_inverse.shape[1]
    vm = pl.BlockSpec(memory_space=pltpu.VMEM)
    V = pltpu.VMEM
    solved, lifted, fixed, sout = pl.pallas_call(
        whole_kernel,
        out_shape=(
            pltpu.VMEM((rows, n), F32),
            pltpu.VMEM((rows, 2 * br), BF16),
            pltpu.VMEM((br, 2 * n), BF16),
            pltpu.VMEM(sep_rhs.shape, F32),
        ),
        in_specs=[pl.BlockSpec(memory_space=pltpu.HBM)] * 8,
        out_specs=(vm, vm, vm, vm),
        scratch_shapes=[
            V(leaf_rhs.shape, F32), V(leaf_inverse.shape, F32), V(leaf_blocks.shape, F32),
            pltpu.SMEM(leaf_pattern.shape, jnp.int32),
            V(leaf_coupling.shape, F32), V(sep_rhs.shape, F32),
            V((rows, rows), BF16), V((rows, rows), BF16),
            V((n + br, rows), BF16), V((n + br, rows), BF16),
            V(leaf_coupling.shape, BF16), V(leaf_coupling.shape, BF16),
            V((2, 2, 2, 2, r1, tile), F32),
            V((2, 2, 2, 2, r1, tile), F32),
            V((2, 2, 2, 2, 2, r2, tile), F32),
            V((sep, sep), BF16), V((sep, sep), BF16),
            V((sep, sep), BF16), V((sep, sep), BF16),
            V((sep, sep), BF16), V((sep, sep), BF16),
            V((sep, n), F32),
            V((2, 2, 2, 2, w, half), F32),
            V((2, 2, 2, w, half), F32),
            V((2, 2, 2, w, half), F32),
            V((2, 2, w, half), F32),
            V((w, sep), F32), V((w, sep), F32),
            V((2, 2, 2, 2, w, half), F32),
            V((2 * r2, n), F32),
            pltpu.SemaphoreType.DMA((64,)),
            pltpu.SemaphoreType.DMA((64,)),
            pltpu.SemaphoreType.DMA((16,)),
        ],
        compiler_params=pltpu.CompilerParams(
            collective_id=0, has_side_effects=True, vmem_limit_bytes=65_800_000
        ),
    )(leaf_rhs, leaf_inverse, leaf_blocks, leaf_pattern, leaf_coupling, sep_rhs, sep_inverse, sep_coupling)

    return pl.pallas_call(
        finish_kernel,
        out_shape=(
            jax.ShapeDtypeStruct((rows, n), F32),
            jax.ShapeDtypeStruct(sep_rhs.shape, F32),
        ),
        in_specs=[vm] * 4,
        out_specs=[pl.BlockSpec(memory_space=pl.ANY)] * 2,
        scratch_shapes=[V((rows, n), F32), pltpu.SemaphoreType.DMA((16,))],
        compiler_params=pltpu.CompilerParams(vmem_limit_bytes=8 * 1024 * 1024),
    )(solved, lifted, fixed, sout)


def finish_kernel(solved, lifted, fixed, sout, out_far, sout_far, out, near):
    br = fixed.shape[0]
    copies = [pltpu.make_async_copy(sout, sout_far, near.at[0])]
    copies[0].start()
    both = fixed[...]
    for i in range(solved.shape[0] // br):
        rows = slice(i * br, (i + 1) * br)
        out[rows, :] = solved[rows, :] - wide(lifted[rows, 0:br], lifted[rows, br : 2 * br], both)
        copy = pltpu.make_async_copy(out.at[pl.ds(i * br, br)], out_far.at[pl.ds(i * br, br)], near.at[i + 1])
        copy.start()
        copies.append(copy)
    for copy in copies:
        copy.wait()


def pick(*args):
    leaf_rhs, leaf_inverse, _, _, leaf_coupling, _, sep_inverse, _ = args
    if (
        lax.axis_size("leaf") == 8
        and lax.axis_size("col") == 4
        and leaf_inverse.shape[1] == leaf_rhs.shape[1] == sep_inverse.shape[1]
        and leaf_coupling.shape[1] == 4 * sep_inverse.shape[1]
    ):
        return fused(*args)
    return shards(*args)


def solution(mesh):
    return jax.shard_map(
        pick,
        mesh=mesh,
        in_specs=(
            P("leaf", "col"),
            P("leaf", None, None),
            P("leaf", None, None),
            P("leaf", None),
            P("leaf", None),
            P("leaf", "col"),
            P("leaf", "col"),
            P("leaf", "col"),
        ),
        out_specs=(P("leaf", "col"), P("leaf", "col")),
        check_vma=False,
    )
```

```python
import functools

import jax
import jax.numpy as jnp
from jax import lax
from jax.experimental import pallas as pl
from jax.experimental.pallas import tpu as pltpu
from jax.sharding import PartitionSpec as P

HIGH = lax.Precision.HIGHEST
F32 = jnp.float32
BF16 = jnp.bfloat16
NN = ((1,), (0,))
NT = ((1,), (1,))


def from_partner(shard, axis, apart):
    return lax.ppermute(shard, axis, [(i, i ^ 1 << apart) for i in range(lax.axis_size(axis))])


def product(left_side, right_side):
    return jnp.dot(left_side, right_side, precision=HIGH, preferred_element_type=jnp.float32)


def product_first(left_side, right_side):
    return lax.dot_general(
        left_side,
        right_side,
        (((0,), (0,)), ((), ())),
        precision=HIGH,
        preferred_element_type=jnp.float32,
    )


def group_sizes(leaf_count):
    result = []
    for level_index in range(1, 5):
        group_span = 4**level_index
        if group_span // 4 < leaf_count:
            result.append(min(group_span, leaf_count))
    return result


def group_total(partial_value, group_size):
    bit_count = group_size.bit_length() - 1
    for bit_place in range(bit_count):
        partial_value = partial_value + from_partner(partial_value, "leaf", bit_place)
    return partial_value


def shards(
    leaf_rhs,
    leaf_inverse,
    leaf_blocks,
    leaf_pattern,
    leaf_coupling,
    sep_rhs,
    sep_inverse,
    sep_coupling,
):
    inverse_full, coupling_full = (
        lax.all_gather(sep_inverse, "col", axis=1, tiled=True),
        lax.all_gather(sep_coupling, "col", axis=1, tiled=True),
    )
    leaf_count = lax.axis_size("leaf")
    position = lax.axis_index("leaf")
    block_count = leaf_inverse.shape[0]
    block_rows = leaf_inverse.shape[1]
    columns = leaf_rhs.shape[1]
    sep_rows = inverse_full.shape[1]
    weighted = leaf_blocks * leaf_pattern[0].astype(jnp.float32)[:, None, None]
    rhs_blocks = leaf_rhs.reshape(block_count, block_rows, columns)
    column_starts = []
    running = 0
    for column_index in range(block_count):
        column_starts.append(running)
        running = running + block_count - 1 - column_index
    pending = [rhs_blocks[i] for i in range(block_count)]
    forward = []
    for column_index in range(block_count):
        solved = product(leaf_inverse[column_index], pending[column_index])
        forward.append(solved)
        below_count = block_count - 1 - column_index
        if below_count:
            pair_start = column_starts[column_index]
            column_blocks = weighted[pair_start : pair_start + below_count].reshape(
                below_count * block_rows, block_rows
            )
            update = product(column_blocks, solved).reshape(below_count, block_rows, columns)
            for later_index in range(below_count):
                pending[column_index + 1 + later_index] = (
                    pending[column_index + 1 + later_index] - update[later_index]
                )
    sizes_list = group_sizes(leaf_count)
    level_total = len(sizes_list)
    row_counts = [sep_rows // size_item for size_item in sizes_list]
    offsets = []
    running = 0
    for row_count in row_counts:
        offsets.append(running)
        running = running + row_count
    last_block = forward[-1]
    level_pieces = []
    for level_index in range(level_total):
        group_size = sizes_list[level_index]
        row_count = row_counts[level_index]
        row_offset = offsets[level_index]
        row_start = position % group_size * row_count
        coupling_rows = leaf_coupling[level_index * block_rows : (level_index + 1) * block_rows]
        partial_value = -product_first(coupling_rows, last_block)
        if level_index > 0:
            child_offset = offsets[level_index - 1]
            child_count = row_counts[level_index - 1]
            partial_value = partial_value - product_first(
                coupling_full[child_offset : child_offset + child_count], level_pieces[-1]
            )
        own_rows = (
            lax.dynamic_slice_in_dim(partial_value, row_start, row_count, 0)
            + sep_rhs[row_offset : row_offset + row_count]
        )
        partial_value = lax.dynamic_update_slice_in_dim(partial_value, own_rows, row_start, 0)
        summed = group_total(partial_value, group_size)
        level_pieces.append(product(inverse_full[row_offset : row_offset + row_count], summed))
    correction = jnp.zeros((block_rows, columns), jnp.float32)
    solution_pieces = [None] * level_total
    parent_full = None
    for level_index in reversed(range(level_total)):
        group_size = sizes_list[level_index]
        row_count = row_counts[level_index]
        row_offset = offsets[level_index]
        row_start = position % group_size * row_count
        target = level_pieces[level_index]
        if parent_full is not None:
            target = target - product(
                coupling_full[row_offset : row_offset + row_count], parent_full
            )
        partial_value = product_first(inverse_full[row_offset : row_offset + row_count], target)
        parent_full = group_total(partial_value, group_size)
        solution_pieces[level_index] = lax.dynamic_slice_in_dim(
            parent_full, row_start, row_count, 0
        )
        correction = correction + product(
            leaf_coupling[level_index * block_rows : (level_index + 1) * block_rows], parent_full
        )
    pending = list(forward)
    pending[-1] = pending[-1] - correction
    backward = [None] * block_count
    for column_index in reversed(range(block_count)):
        target = pending[column_index]
        below_count = block_count - 1 - column_index
        if below_count:
            pair_start = column_starts[column_index]
            column_blocks = weighted[pair_start : pair_start + below_count].reshape(
                below_count * block_rows, block_rows
            )
            later_blocks = jnp.concatenate(backward[column_index + 1 :], 0)
            target = target - product_first(column_blocks, later_blocks)
        backward[column_index] = product_first(leaf_inverse[column_index], target)
    return (jnp.concatenate(backward, 0), jnp.concatenate(solution_pieces, 0))


def halves(value):
    top = value.astype(BF16)
    return top, (value - top.astype(F32)).astype(BF16)


def mm(left_side, right_side, dims=NN):
    return lax.dot_general(
        left_side, right_side, (dims, ((), ())), preferred_element_type=F32
    )


def wide(left_top, left_low, right_both):
    n = right_both.shape[1] // 2
    both = mm(left_top, right_both)
    return both[:, :n] + both[:, n:] + mm(left_low, right_both[:, :n])


def tall(left_side, right_top, right_low, dims=NN):
    n = left_side.shape[0]
    top, low = halves(left_side)
    both = mm(jnp.concatenate([top, low], 0), right_top, dims)
    return both[:n] + both[n:] + mm(top, right_low, dims)


def tall3(left_top, left_low, right_top, right_low, dims=NN):
    n = left_top.shape[0]
    both = mm(jnp.concatenate([left_top, left_low], 0), right_top, dims)
    return both[:n] + both[n:] + mm(left_top, right_low, dims)


def whole_kernel(
    rhs_far, inv_far, blk_far, pat_far, cpl_far, srhs_far, sinv, scpl,
    solved, lifted, fixed, sout,
    rhs, inv, blk, pat, cpl, srhs,
    l_top, l_low, xt_top, xt_low,
    e_top, e_low, d1b, cb, d2b, d1_top, d1_low, c_top, c_low, d2_top, d2_low,
    pad, part, ra, acc, rb, tsend, trecv, xg, tmp, u_top, u_low, v_top, v_low, gauge, send, recv, near,
):
    leaf = lax.axis_index("leaf")
    col = lax.axis_index("col")
    y = lax.rem(leaf, 2)
    z0 = lax.rem(lax.div(leaf, 2), 2)
    z1 = lax.div(leaf, 4)
    core = lax.rem(col, 2)
    x = lax.div(col, 2)
    to_core = (leaf, col + 1 - 2 * core)
    to_x = (leaf, col + 2 - 4 * x)
    to_y = (leaf + 1 - 2 * y, col)
    to_z0 = (leaf + 2 - 4 * z0, col)
    to_z1 = (leaf + 4 - 8 * z1, col)

    barrier = pltpu.get_barrier_semaphore()
    partners = (to_core, to_x, to_y, to_z0, to_z1)
    for partner in partners:
        pl.semaphore_signal(
            barrier, inc=1, device_id=partner, device_id_type=pl.DeviceIdType.MESH
        )
    nb, br = inv.shape[0], inv.shape[1]
    n = rhs.shape[1]
    sep = cpl.shape[1]
    half = sep // 2
    r1, r2 = sep // 4, sep // 8
    w = n // 4
    starts = []
    running = 0
    for j in range(nb):
        starts.append(running)
        running += nb - 1 - j

    def rows_of(ref):
        count = 1
        for size in ref.shape:
            count *= size
        return count // 128

    def land(semaphore, count):
        box = gauge.at[pl.ds(0, count)]
        pltpu.make_async_copy(box, box, semaphore).wait()

    loads = []

    def fetch(*pairs):
        semaphore = near.at[len(loads)]
        loads.append(semaphore)
        count = 0
        for src, dst in pairs:
            pltpu.make_async_copy(src, dst, semaphore).start()
            count += rows_of(dst)
        return semaphore, count

    pat_copy = pltpu.make_async_copy(pat_far, pat, near.at[0])
    pat_copy.start()
    loads.append(near.at[0])
    got_main = fetch((inv_far, inv), (rhs_far, rhs))
    got_blk = []
    for j in range(nb - 1):
        box = pl.ds(starts[j], nb - 1 - j)
        got_blk.append(fetch((blk_far.at[box], blk.at[box])))
    got_own = fetch(
        (sinv.at[pl.ds(0, r1)], d1b.at[z0, y, x, core]),
        (scpl, cb.at[z0, y, x, core]),
        (sinv.at[pl.ds(r1, r2)], d2b.at[z1, z0, y, x, core]),
    )
    got_rest = fetch((cpl_far, cpl), (srhs_far, srhs))

    shipped = []
    groups = []

    def ship(moves):
        semaphore = recv.at[len(groups)]
        groups.append(len(moves))
        count = 0
        for src, dst, target in moves:
            pltpu.make_async_remote_copy(
                src_ref=src, dst_ref=dst, send_sem=send.at[0], recv_sem=semaphore,
                device_id=target, device_id_type=pl.DeviceIdType.MESH,
            ).start()
            count += rows_of(dst)
        shipped.append(count)
        return semaphore, count

    def arrived(sent):
        land(*sent)

    partner_of = {"x": to_x, "y": to_y, "z": to_z0}
    place_of = {"x": x, "y": y, "z": z0}
    order_1 = (("xyz", 3), ("yzx", 3), ("zxy", 2))
    order_c = (("yzx", 5), ("zyx", 5), ("xyz", 3), ("xzy", 3))
    order_2 = (("xyz", 3), ("yzx", 3), ("zxy", 2))
    every = (slice(None),)

    def row_parts(count, orders):
        units = count // 8
        weight = sum(share for _, share in orders)
        result = []
        begin = seen = 0
        for order, share in orders:
            seen += share
            end = seen * units // weight * 8
            result.append((order, begin, end - begin))
            begin = end
        return result

    def boxes(ref, orders, step, lead, fresh):
        result = []
        for order, begin, size in row_parts(ref.shape[-2], orders):
            have = order[:step]
            where = []
            for name in "zyx":
                if fresh and name == order[step - 1]:
                    where.append(1 - place_of[name])
                elif name in have:
                    where.append(slice(None))
                else:
                    where.append(place_of[name])
            result.append((order, ref.at[lead + tuple(where) + (core, pl.ds(begin, size))], begin, size))
        return result

    def stage(ref, orders, step, source=None, lead=()):
        sent = []
        for order, box, begin, size in boxes(ref, orders, step, lead, False):
            src = box if source is None else source.at[pl.ds(begin, size)]
            sent.append((src, box, partner_of[order[step]]))
        return ship(sent)

    def cross(ref, orders, step, lead=(), fresh=False):
        return ship([(box, box, to_core) for _, box, _, _ in boxes(ref, orders, step, lead, fresh)])

    def at(i):
        return slice(i * br, (i + 1) * br)

    def load_column(j):
        if j < nb - 1:
            land(*got_blk[j])
        l_top[at(j), at(j)], l_low[at(j), at(j)] = halves(inv[j])
        for i in range(j + 1, nb):
            p = starts[j] + i - j - 1
            block = blk[p] * pat[0, p].astype(F32)
            l_top[at(i), at(j)], l_low[at(i), at(j)] = halves(block)

    pending = []
    forward = [None] * nb

    def begin_forward():
        pat_copy.wait()
        land(*got_main)
        pending.extend(rhs[at(i)] for i in range(nb))

    def forward_step(j):
        load_column(j)
        top, low = halves(pending[j])
        solved_j = wide(l_top[at(j), at(j)], l_low[at(j), at(j)], jnp.concatenate([top, low], 1))
        forward[j] = solved_j
        top, low = halves(solved_j)
        both = jnp.concatenate([top, low], 1)
        for i in range(j + 1, nb):
            pending[i] = pending[i] - wide(l_top[at(i), at(j)], l_low[at(i), at(j)], both)

    last_t = []

    def end_forward():
        land(*got_rest)
        e_top[...], e_low[...] = halves(cpl[...])
        last_t.append(forward[nb - 1].T)

    def make_part(l):
        pad[...] = jnp.zeros_like(pad)
        if l == 0:
            pad[pl.ds(pl.multiple_of((2 * z0 + y) * r1, r1), r1), :] = srhs[0:r1]
        else:
            pad[pl.ds(pl.multiple_of(leaf * r2, r2), r2), :] = srhs[r1 : r1 + r2]
        term = pad[...].T - tall(last_t[0], e_top[at(l), :], e_low[at(l), :])
        for h in range(2):
            part[l, h] = term[:, h * half : (h + 1) * half].reshape(2, 2, w, half)

    def send_part(l):
        return (
            ship([(part.at[l, 0, :, 1 - y], ra.at[l, 0], to_y)]),
            ship([(part.at[l, 1, 1 - z0, :], ra.at[l, 1], to_z0)]),
        )

    def second(l, pair):
        arrived(pair[0])
        acc[l, 0] = part[l, 0, :, y] + ra[l, 0]
        first = ship([(acc.at[l, 0, 1 - z0], rb.at[l, 0], to_z0)])
        arrived(pair[1])
        acc[l, 1] = part[l, 1, z0] + ra[l, 1]
        return first, ship([(acc.at[l, 1, 1 - y], rb.at[l, 1], to_y)])

    def total(l, pair):
        arrived(pair[0])
        arrived(pair[1])
        return jnp.concatenate([acc[l, 0, z0] + rb[l, 0], acc[l, 1, y] + rb[l, 1]], 1)

    row = lax.broadcasted_iota(jnp.int32, (br, br), 0)
    column = lax.broadcasted_iota(jnp.int32, (br, br), 1)
    unit = jnp.where(row == column, 1.0, 0.0).astype(F32)

    def backward_step(i):
        first = forward[i].T
        below = unit if i == nb - 1 else jnp.zeros((br, br), F32)
        target = jnp.concatenate([first, below], 0)
        if i < nb - 1:
            rest = slice((i + 1) * br, nb * br)
            target = target - (
                mm(xt_top[:, rest], l_top[rest, at(i)])
                + mm(xt_low[:, rest], l_top[rest, at(i)])
                + mm(xt_top[:, rest], l_low[rest, at(i)])
            )
        value = tall(target, l_top[at(i), at(i)], l_low[at(i), at(i)])
        xt_top[:, at(i)], xt_low[:, at(i)] = halves(value)
        solved[at(i), :] = value[:n].T
        top, low = halves(value[n:].T)
        lifted[at(i), 0:br] = top
        lifted[at(i), br : 2 * br] = low

    def spread(src, top_ref, low_ref, rows, lead):
        for k in range(lead):
            for c in range(4):
                if lead == 4:
                    tile = src[k // 2, k % 2, c // 2, c % 2]
                else:
                    tile = src[k // 4, k // 2 % 2, k % 2, c // 2, c % 2]
                where = (slice(k * rows, (k + 1) * rows), slice(c * tile.shape[1], (c + 1) * tile.shape[1]))
                top, low = halves(tile)
                top_ref[where] = top
                low_ref[where] = low

    def give(l, value):
        xg[l, 0, z0, y] = value[:, :half]
        xg[l, 1, z0, y] = value[:, half:]
        return (
            ship([(xg.at[l, 0, z0, y], xg.at[l, 0, z0, y], to_y)]),
            ship([(xg.at[l, 1, z0, y], xg.at[l, 1, z0, y], to_z0)]),
        )

    def give_more(l, pair):
        arrived(pair[0])
        first = ship([(xg.at[l, 0, z0], xg.at[l, 0, z0], to_z0)])
        arrived(pair[1])
        return first, ship([(xg.at[l, 1, :, y], xg.at[l, 1, :, y], to_y)])

    def against(top_ref, low_ref, l, h):
        top, low = halves(xg[l, h].reshape(n, half))
        lanes = slice(h * half, (h + 1) * half)
        left = jnp.concatenate([top_ref[:, lanes], low_ref[:, lanes]], 0)
        both = mm(left, top, NT)
        return both[: 2 * br] + both[2 * br :] + mm(top_ref[:, lanes], low, NT)

    def make_u():
        tile = pl.ds(pl.multiple_of((2 * z0 + y) * r1, r1), r1)
        u_top[0:br, :], u_low[0:br, :] = halves(tall3(e_top[at(0), :], e_low[at(0), :], d1_top[...], d1_low[...], NT))
        u_top[br : 2 * br, :] = d1_top[:, tile].T
        u_low[br : 2 * br, :] = d1_low[:, tile].T

    def make_v():
        value = tall3(u_top[...], u_low[...], c_top[...], c_low[...], NN)
        v_top[0:br, :], v_low[0:br, :] = halves(cpl[at(1), :] - value[0:br])
        v_top[br : 2 * br, :], v_low[br : 2 * br, :] = halves(-value[br : 2 * br])

    begin_forward()
    forward_step(0)
    forward_step(1)
    pl.semaphore_wait(barrier, len(partners))
    d1_a = stage(d1b, order_1, 0, sinv)
    c_a = stage(cb, order_c, 0, scpl)
    d2_z = ship([(sinv.at[pl.ds(r1, r2)], d2b.at[z1, z0, y, x, core], to_z1)])
    forward_step(2)
    forward_step(3)
    forward_step(4)
    forward_step(5)
    land(*got_own)
    arrived(d1_a)
    d1_b = stage(d1b, order_1, 1)
    forward_step(6)
    end_forward()
    make_part(0)
    a1 = send_part(0)
    arrived(c_a)
    c_b = stage(cb, order_c, 1)
    make_part(1)
    backward_step(6)
    arrived(d1_b)
    d1_c = stage(d1b, order_1, 2)
    d1_d = cross(d1b, order_1, 2)
    b1 = second(0, a1)
    a2 = send_part(1)
    arrived(c_b)
    c_c = stage(cb, order_c, 2)
    c_d = cross(cb, order_c, 2)
    arrived(d2_z)
    d2_a = stage(d2b, order_2, 0, lead=every)
    backward_step(5)
    backward_step(4)
    arrived(d1_c)
    d1_e = cross(d1b, order_1, 3, fresh=True)
    b2 = second(1, a2)
    backward_step(3)
    arrived(d1_d)
    arrived(d1_e)
    spread(d1b, d1_top, d1_low, r1, 4)
    s_1 = total(0, b1)
    z_1 = tall(s_1, d1_top[...], d1_low[...], NT)
    arrived(c_c)
    c_e = cross(cb, order_c, 3, fresh=True)
    arrived(d2_a)
    d2_b = stage(d2b, order_2, 1, lead=every)
    make_u()
    arrived(c_d)
    arrived(c_e)
    spread(cb, c_top, c_low, r1, 4)
    s_2 = total(1, b2)
    tsend[...] = s_2 - tall(z_1, c_top[...], c_low[...])
    ts = ship([(tsend, trecv, to_z1)])
    g1 = give(0, z_1)
    arrived(d2_b)
    d2_c = stage(d2b, order_2, 2, lead=every)
    d2_d = cross(d2b, order_2, 2, lead=every)
    make_v()
    g1 = give_more(0, g1)
    backward_step(2)
    backward_step(1)
    arrived(d2_c)
    d2_e = cross(d2b, order_2, 3, lead=every, fresh=True)
    backward_step(0)
    arrived(d2_d)
    arrived(d2_e)
    spread(d2b, d2_top, d2_low, r2, 8)
    arrived(ts)
    z_2 = tall(tsend[...] + trecv[...], d2_top[...], d2_low[...], NT)
    x_2 = tall(z_2, d2_top[...], d2_low[...])
    g2 = give(1, x_2)
    arrived(g1[0])
    arrived(g1[1])
    base = against(u_top, u_low, 0, 0) + against(u_top, u_low, 0, 1)
    g2 = give_more(1, g2)
    arrived(g2[0])
    base = base + against(v_top, v_low, 1, 0)
    arrived(g2[1])
    base = base + against(v_top, v_low, 1, 1)
    top, low = halves(base[0:br])
    fixed[...] = jnp.concatenate([top, low], 1)
    sout[0:r1, :] = base[br : 2 * br]
    tmp[...] = xg[1, z1, :, :, :, pl.ds(pl.multiple_of(z0 * 2 * r2, 2 * r2), 2 * r2)].reshape(n, 2 * r2).T
    sout[r1 : r1 + r2, :] = tmp[pl.ds(pl.multiple_of(y * r2, r2), r2), :]
    land(send.at[0], sum(shipped))


def fused(leaf_rhs, leaf_inverse, leaf_blocks, leaf_pattern, leaf_coupling, sep_rhs, sep_inverse, sep_coupling):
    rows, n = leaf_rhs.shape
    br = leaf_inverse.shape[1]
    sep = leaf_coupling.shape[1]
    half, w = sep // 2, n // 4
    r1, r2 = sep // 4, sep // 8
    tile = sep_inverse.shape[1]
    vm = pl.BlockSpec(memory_space=pltpu.VMEM)
    V = pltpu.VMEM
    solved, lifted, fixed, sout = pl.pallas_call(
        whole_kernel,
        out_shape=(
            pltpu.VMEM((rows, n), F32),
            pltpu.VMEM((rows, 2 * br), BF16),
            pltpu.VMEM((br, 2 * n), BF16),
            pltpu.VMEM(sep_rhs.shape, F32),
        ),
        in_specs=[pl.BlockSpec(memory_space=pltpu.HBM)] * 8,
        out_specs=(vm, vm, vm, vm),
        scratch_shapes=[
            V(leaf_rhs.shape, F32), V(leaf_inverse.shape, F32), V(leaf_blocks.shape, F32),
            pltpu.SMEM(leaf_pattern.shape, jnp.int32),
            V(leaf_coupling.shape, F32), V(sep_rhs.shape, F32),
            V((rows, rows), BF16), V((rows, rows), BF16),
            V((n + br, rows), BF16), V((n + br, rows), BF16),
            V(leaf_coupling.shape, BF16), V(leaf_coupling.shape, BF16),
            V((2, 2, 2, 2, r1, tile), F32),
            V((2, 2, 2, 2, r1, tile), F32),
            V((2, 2, 2, 2, 2, r2, tile), F32),
            V((sep, sep), BF16), V((sep, sep), BF16),
            V((sep, sep), BF16), V((sep, sep), BF16),
            V((sep, sep), BF16), V((sep, sep), BF16),
            V((sep, n), F32),
            V((2, 2, 2, 2, w, half), F32),
            V((2, 2, 2, w, half), F32),
            V((2, 2, 2, w, half), F32),
            V((2, 2, w, half), F32),
            V((w, sep), F32), V((w, sep), F32),
            V((2, 2, 2, 2, w, half), F32),
            V((2 * r2, n), F32),
            V((2 * br, sep), BF16), V((2 * br, sep), BF16),
            V((2 * br, sep), BF16), V((2 * br, sep), BF16),
            V((12 * 1024, 128), F32),
            pltpu.SemaphoreType.DMA((1,)),
            pltpu.SemaphoreType.DMA((34,)),
            pltpu.SemaphoreType.DMA((10,)),
        ],
        compiler_params=pltpu.CompilerParams(
            collective_id=0, has_side_effects=True, vmem_limit_bytes=65_800_000
        ),
    )(leaf_rhs, leaf_inverse, leaf_blocks, leaf_pattern, leaf_coupling, sep_rhs, sep_inverse, sep_coupling)

    return pl.pallas_call(
        finish_kernel,
        out_shape=(
            jax.ShapeDtypeStruct((rows, n), F32),
            jax.ShapeDtypeStruct(sep_rhs.shape, F32),
        ),
        in_specs=[vm] * 4,
        out_specs=[pl.BlockSpec(memory_space=pl.ANY)] * 2,
        scratch_shapes=[V((rows, n), F32), pltpu.SemaphoreType.DMA((2,))],
        compiler_params=pltpu.CompilerParams(vmem_limit_bytes=8 * 1024 * 1024),
    )(solved, lifted, fixed, sout)


def finish_kernel(solved, lifted, fixed, sout, out_far, sout_far, out, near):
    br = fixed.shape[0]
    sep_copy = pltpu.make_async_copy(sout, sout_far, near.at[0])
    sep_copy.start()
    both = fixed[...]
    for i in range(solved.shape[0] // br):
        rows = slice(i * br, (i + 1) * br)
        out[rows, :] = solved[rows, :] - wide(lifted[rows, 0:br], lifted[rows, br : 2 * br], both)
        pltpu.make_async_copy(out.at[pl.ds(i * br, br)], out_far.at[pl.ds(i * br, br)], near.at[1]).start()
    sep_copy.wait()
    pltpu.make_async_copy(out, out_far, near.at[1]).wait()


def pick(*args):
    leaf_rhs, leaf_inverse, _, _, leaf_coupling, _, sep_inverse, _ = args
    if (
        lax.axis_size("leaf") == 8
        and lax.axis_size("col") == 4
        and leaf_inverse.shape[1] == leaf_rhs.shape[1] == sep_inverse.shape[1]
        and leaf_coupling.shape[1] == 4 * sep_inverse.shape[1]
    ):
        return fused(*args)
    return shards(*args)


def solution(mesh):
    return jax.shard_map(
        pick,
        mesh=mesh,
        in_specs=(
            P("leaf", "col"),
            P("leaf", None, None),
            P("leaf", None, None),
            P("leaf", None),
            P("leaf", None),
            P("leaf", "col"),
            P("leaf", "col"),
            P("leaf", "col"),
        ),
        out_specs=(P("leaf", "col"), P("leaf", "col")),
        check_vma=False,
    )
```

```python
import functools

import jax
import jax.numpy as jnp
from jax import lax
from jax.experimental import pallas as pl
from jax.experimental.pallas import tpu as pltpu
from jax.sharding import PartitionSpec as P

HIGH = lax.Precision.HIGHEST
F32 = jnp.float32
BF16 = jnp.bfloat16
NN = ((1,), (0,))
NT = ((1,), (1,))


def from_partner(shard, axis, apart):
    return lax.ppermute(shard, axis, [(i, i ^ 1 << apart) for i in range(lax.axis_size(axis))])


def product(left_side, right_side):
    return jnp.dot(left_side, right_side, precision=HIGH, preferred_element_type=jnp.float32)


def product_first(left_side, right_side):
    return lax.dot_general(
        left_side,
        right_side,
        (((0,), (0,)), ((), ())),
        precision=HIGH,
        preferred_element_type=jnp.float32,
    )


def group_sizes(leaf_count):
    result = []
    for level_index in range(1, 5):
        group_span = 4**level_index
        if group_span // 4 < leaf_count:
            result.append(min(group_span, leaf_count))
    return result


def group_total(partial_value, group_size):
    bit_count = group_size.bit_length() - 1
    for bit_place in range(bit_count):
        partial_value = partial_value + from_partner(partial_value, "leaf", bit_place)
    return partial_value


def shards(
    leaf_rhs,
    leaf_inverse,
    leaf_blocks,
    leaf_pattern,
    leaf_coupling,
    sep_rhs,
    sep_inverse,
    sep_coupling,
):
    inverse_full, coupling_full = (
        lax.all_gather(sep_inverse, "col", axis=1, tiled=True),
        lax.all_gather(sep_coupling, "col", axis=1, tiled=True),
    )
    leaf_count = lax.axis_size("leaf")
    position = lax.axis_index("leaf")
    block_count = leaf_inverse.shape[0]
    block_rows = leaf_inverse.shape[1]
    columns = leaf_rhs.shape[1]
    sep_rows = inverse_full.shape[1]
    weighted = leaf_blocks * leaf_pattern[0].astype(jnp.float32)[:, None, None]
    rhs_blocks = leaf_rhs.reshape(block_count, block_rows, columns)
    column_starts = []
    running = 0
    for column_index in range(block_count):
        column_starts.append(running)
        running = running + block_count - 1 - column_index
    pending = [rhs_blocks[i] for i in range(block_count)]
    forward = []
    for column_index in range(block_count):
        solved = product(leaf_inverse[column_index], pending[column_index])
        forward.append(solved)
        below_count = block_count - 1 - column_index
        if below_count:
            pair_start = column_starts[column_index]
            column_blocks = weighted[pair_start : pair_start + below_count].reshape(
                below_count * block_rows, block_rows
            )
            update = product(column_blocks, solved).reshape(below_count, block_rows, columns)
            for later_index in range(below_count):
                pending[column_index + 1 + later_index] = (
                    pending[column_index + 1 + later_index] - update[later_index]
                )
    sizes_list = group_sizes(leaf_count)
    level_total = len(sizes_list)
    row_counts = [sep_rows // size_item for size_item in sizes_list]
    offsets = []
    running = 0
    for row_count in row_counts:
        offsets.append(running)
        running = running + row_count
    last_block = forward[-1]
    level_pieces = []
    for level_index in range(level_total):
        group_size = sizes_list[level_index]
        row_count = row_counts[level_index]
        row_offset = offsets[level_index]
        row_start = position % group_size * row_count
        coupling_rows = leaf_coupling[level_index * block_rows : (level_index + 1) * block_rows]
        partial_value = -product_first(coupling_rows, last_block)
        if level_index > 0:
            child_offset = offsets[level_index - 1]
            child_count = row_counts[level_index - 1]
            partial_value = partial_value - product_first(
                coupling_full[child_offset : child_offset + child_count], level_pieces[-1]
            )
        own_rows = (
            lax.dynamic_slice_in_dim(partial_value, row_start, row_count, 0)
            + sep_rhs[row_offset : row_offset + row_count]
        )
        partial_value = lax.dynamic_update_slice_in_dim(partial_value, own_rows, row_start, 0)
        summed = group_total(partial_value, group_size)
        level_pieces.append(product(inverse_full[row_offset : row_offset + row_count], summed))
    correction = jnp.zeros((block_rows, columns), jnp.float32)
    solution_pieces = [None] * level_total
    parent_full = None
    for level_index in reversed(range(level_total)):
        group_size = sizes_list[level_index]
        row_count = row_counts[level_index]
        row_offset = offsets[level_index]
        row_start = position % group_size * row_count
        target = level_pieces[level_index]
        if parent_full is not None:
            target = target - product(
                coupling_full[row_offset : row_offset + row_count], parent_full
            )
        partial_value = product_first(inverse_full[row_offset : row_offset + row_count], target)
        parent_full = group_total(partial_value, group_size)
        solution_pieces[level_index] = lax.dynamic_slice_in_dim(
            parent_full, row_start, row_count, 0
        )
        correction = correction + product(
            leaf_coupling[level_index * block_rows : (level_index + 1) * block_rows], parent_full
        )
    pending = list(forward)
    pending[-1] = pending[-1] - correction
    backward = [None] * block_count
    for column_index in reversed(range(block_count)):
        target = pending[column_index]
        below_count = block_count - 1 - column_index
        if below_count:
            pair_start = column_starts[column_index]
            column_blocks = weighted[pair_start : pair_start + below_count].reshape(
                below_count * block_rows, block_rows
            )
            later_blocks = jnp.concatenate(backward[column_index + 1 :], 0)
            target = target - product_first(column_blocks, later_blocks)
        backward[column_index] = product_first(leaf_inverse[column_index], target)
    return (jnp.concatenate(backward, 0), jnp.concatenate(solution_pieces, 0))


def halves(value):
    top = value.astype(BF16)
    return top, (value - top.astype(F32)).astype(BF16)


def mm(left_side, right_side, dims=NN):
    return lax.dot_general(
        left_side, right_side, (dims, ((), ())), preferred_element_type=F32
    )


def wide(left_top, left_low, right_both):
    n = right_both.shape[1] // 2
    both = mm(left_top, right_both)
    return both[:, :n] + both[:, n:] + mm(left_low, right_both[:, :n])


def tall(left_side, right_top, right_low, dims=NN):
    n = left_side.shape[0]
    top, low = halves(left_side)
    both = mm(jnp.concatenate([top, low], 0), right_top, dims)
    return both[:n] + both[n:] + mm(top, right_low, dims)


def tall3(left_top, left_low, right_top, right_low, dims=NN):
    n = left_top.shape[0]
    both = mm(jnp.concatenate([left_top, left_low], 0), right_top, dims)
    return both[:n] + both[n:] + mm(left_top, right_low, dims)


def whole_kernel(
    rhs_far, inv_far, blk_far, pat_far, cpl_far, srhs_far, sinv, scpl,
    solved, lifted, fixed, sout,
    rhs, inv, blk, pat, cpl, srhs,
    l_top, l_low, xt_top, xt_low,
    e_top, e_low, d1b, cb, d2b, d1_top, d1_low, c_top, c_low, d2_top, d2_low,
    pad, part, ra, acc, rb, tsend, trecv, xg, tmp, u_top, u_low, v_top, v_low, gauge, send, recv, near,
):
    leaf = lax.axis_index("leaf")
    col = lax.axis_index("col")
    y = lax.rem(leaf, 2)
    z0 = lax.rem(lax.div(leaf, 2), 2)
    z1 = lax.div(leaf, 4)
    core = lax.rem(col, 2)
    x = lax.div(col, 2)
    to_core = (leaf, col + 1 - 2 * core)
    to_x = (leaf, col + 2 - 4 * x)
    to_y = (leaf + 1 - 2 * y, col)
    to_z0 = (leaf + 2 - 4 * z0, col)
    to_z1 = (leaf + 4 - 8 * z1, col)

    barrier = pltpu.get_barrier_semaphore()
    to_yz = (leaf + 1 - 2 * y + 2 - 4 * z0, col)
    partners = (to_core, to_x, to_y, to_z0, to_z1, to_yz)
    for partner in partners:
        pl.semaphore_signal(
            barrier, inc=1, device_id=partner, device_id_type=pl.DeviceIdType.MESH
        )
    nb, br = inv.shape[0], inv.shape[1]
    n = rhs.shape[1]
    sep = cpl.shape[1]
    half = sep // 2
    r1, r2 = sep // 4, sep // 8
    w = n // 4
    starts = []
    running = 0
    for j in range(nb):
        starts.append(running)
        running += nb - 1 - j

    def rows_of(ref):
        count = 1
        for size in ref.shape:
            count *= size
        return count // 128

    def land(semaphore, count):
        box = gauge.at[pl.ds(0, count)]
        pltpu.make_async_copy(box, box, semaphore).wait()

    loads = []

    def fetch(*pairs):
        semaphore = near.at[len(loads)]
        loads.append(semaphore)
        count = 0
        for src, dst in pairs:
            pltpu.make_async_copy(src, dst, semaphore).start()
            count += rows_of(dst)
        return semaphore, count

    pat_copy = pltpu.make_async_copy(pat_far, pat, near.at[0])
    pat_copy.start()
    loads.append(near.at[0])
    got_main = fetch((inv_far, inv), (rhs_far, rhs))
    got_blk = []
    for begin, end in ((0, starts[1]), (starts[1], running)):
        box = pl.ds(begin, end - begin)
        got_blk.append(fetch((blk_far.at[box], blk.at[box])))
    got_own = fetch(
        (sinv.at[pl.ds(0, r1)], d1b.at[z0, y, x, core]),
        (scpl, cb.at[z0, y, x, core]),
        (sinv.at[pl.ds(r1, r2)], d2b.at[z1, z0, y, x, core]),
    )
    got_rest = fetch((cpl_far, cpl), (srhs_far, srhs))

    shipped = []
    groups = []

    def begin_moves(semaphore, moves):
        count = 0
        for src, dst, target in moves:
            pltpu.make_async_remote_copy(
                src_ref=src, dst_ref=dst, send_sem=send.at[0], recv_sem=semaphore,
                device_id=target, device_id_type=pl.DeviceIdType.MESH,
            ).start()
            count += rows_of(dst)
        shipped.append(count)
        return count

    def ship(moves):
        semaphore = recv.at[len(groups)]
        groups.append(len(moves))
        return semaphore, begin_moves(semaphore, moves)

    def more(sent, moves):
        return sent[0], sent[1] + begin_moves(sent[0], moves)

    def arrived(sent):
        land(*sent)

    partner_of = {"x": to_x, "y": to_y, "z": to_z0}
    place_of = {"x": x, "y": y, "z": z0}
    order_1 = (("yzx", 3), ("zyx", 3), ("xyz", 1), ("xzy", 1))
    order_c = (("yzx", 5), ("zyx", 5), ("xyz", 3), ("xzy", 3))
    order_2 = (("yzx", 5), ("zyx", 5), ("xyz", 3), ("xzy", 3))
    every = (slice(None),)

    def row_parts(count, orders):
        units = count // 8
        weight = sum(share for _, share in orders)
        result = []
        begin = seen = 0
        for order, share in orders:
            seen += share
            end = seen * units // weight * 8
            result.append((order, begin, end - begin))
            begin = end
        return result

    def tile(ref, lead, begin, size, far):
        where = tuple(1 - place_of[name] if name in far else place_of[name] for name in "zyx")
        return ref.at[lead + where + (core, pl.ds(begin, size))]

    def first_wave(ref, orders, lead=()):
        near_moves, last_moves = [], []
        parts = row_parts(ref.shape[-2], orders)
        for k in range(3):
            for order, begin, size in parts:
                box = tile(ref, lead, begin, size, "")
                move = (box, box, partner_of[order[k]])
                (last_moves if k == 2 else near_moves).append(move)
        started = ship(near_moves)
        last = ship(last_moves)
        return started, last

    def second_wave(ref, orders, sent, lead=()):
        near_moves, last_moves = [], []
        for order, begin, size in row_parts(ref.shape[-2], orders):
            p, q, r = order
            box = tile(ref, lead, begin, size, p)
            near_moves.append((box, box, partner_of[q]))
            last_moves.append((box, box, partner_of[r]))
            box = tile(ref, lead, begin, size, q)
            last_moves.append((box, box, partner_of[r]))
        started = ship(near_moves)
        return started, more(sent[1], last_moves)

    def third_wave(ref, orders, sent, lead=()):
        moves = []
        for order, begin, size in row_parts(ref.shape[-2], orders):
            box = tile(ref, lead, begin, size, order[:2])
            moves.append((box, box, partner_of[order[2]]))
        return more(sent[1], moves)

    def cross(ref, orders, fresh, lead=()):
        moves = []
        for order, begin, size in row_parts(ref.shape[-2], orders):
            where = []
            for name in "zyx":
                if name != order[2]:
                    where.append(slice(None))
                else:
                    where.append(1 - place_of[name] if fresh else place_of[name])
            box = ref.at[lead + tuple(where) + (core, pl.ds(begin, size))]
            moves.append((box, box, to_core))
        return ship(moves)

    def at(i):
        return slice(i * br, (i + 1) * br)

    def load_column(j):
        if j < 2:
            land(*got_blk[j])
        l_top[at(j), at(j)], l_low[at(j), at(j)] = halves(inv[j])
        for i in range(j + 1, nb):
            p = starts[j] + i - j - 1
            block = blk[p] * pat[0, p].astype(F32)
            l_top[at(i), at(j)], l_low[at(i), at(j)] = halves(block)

    pending = []
    forward = [None] * nb

    def begin_forward():
        pat_copy.wait()
        land(*got_main)
        pending.extend(rhs[at(i)] for i in range(nb))

    def forward_step(j):
        load_column(j)
        top, low = halves(pending[j])
        solved_j = wide(l_top[at(j), at(j)], l_low[at(j), at(j)], jnp.concatenate([top, low], 1))
        forward[j] = solved_j
        top, low = halves(solved_j)
        both = jnp.concatenate([top, low], 1)
        for i in range(j + 1, nb):
            pending[i] = pending[i] - wide(l_top[at(i), at(j)], l_low[at(i), at(j)], both)

    last_t = []

    def end_forward():
        land(*got_rest)
        e_top[...], e_low[...] = halves(cpl[...])
        last_t.append(forward[nb - 1].T)

    def make_part(l):
        pad[...] = jnp.zeros_like(pad)
        if l == 0:
            pad[pl.ds(pl.multiple_of((2 * z0 + y) * r1, r1), r1), :] = srhs[0:r1]
        else:
            pad[pl.ds(pl.multiple_of(leaf * r2, r2), r2), :] = srhs[r1 : r1 + r2]
        term = pad[...].T - tall(last_t[0], e_top[at(l), :], e_low[at(l), :])
        for h in range(2):
            part[l, h] = term[:, h * half : (h + 1) * half].reshape(2, 2, w, half)

    def send_part(l):
        first = ship([(part.at[l, 0, 1 - z0, 1 - y], ra.at[l, 0, 0], to_y)])
        other = ship([(part.at[l, 1, 1 - z0, 1 - y], ra.at[l, 1, 0], to_z0)])
        last = ship([
            (part.at[l, 0, z0, 1 - y], ra.at[l, 0, 1], to_y),
            (part.at[l, 1, 1 - z0, y], ra.at[l, 1, 1], to_z0),
        ])
        return first, other, last

    def second(l, sent):
        arrived(sent[0])
        acc[l, 0] = part[l, 0, 1 - z0, y] + ra[l, 0, 0]
        last = more(sent[2], [(acc.at[l, 0], rb.at[l, 0], to_z0)])
        arrived(sent[1])
        acc[l, 1] = part[l, 1, z0, 1 - y] + ra[l, 1, 0]
        return more(last, [(acc.at[l, 1], rb.at[l, 1], to_y)])

    def total(l, sent):
        arrived(sent)
        return jnp.concatenate([part[l, h, z0, y] + ra[l, h, 1] + rb[l, h] for h in range(2)], 1)

    row = lax.broadcasted_iota(jnp.int32, (br, br), 0)
    column = lax.broadcasted_iota(jnp.int32, (br, br), 1)
    unit = jnp.where(row == column, 1.0, 0.0).astype(F32)

    def backward_step(i):
        first = forward[i].T
        below = unit if i == nb - 1 else jnp.zeros((br, br), F32)
        target = jnp.concatenate([first, below], 0)
        if i < nb - 1:
            rest = slice((i + 1) * br, nb * br)
            target = target - (
                mm(xt_top[:, rest], l_top[rest, at(i)])
                + mm(xt_low[:, rest], l_top[rest, at(i)])
                + mm(xt_top[:, rest], l_low[rest, at(i)])
            )
        value = tall(target, l_top[at(i), at(i)], l_low[at(i), at(i)])
        xt_top[:, at(i)], xt_low[:, at(i)] = halves(value)
        solved[at(i), :] = value[:n].T
        top, low = halves(value[n:].T)
        lifted[at(i), 0:br] = top
        lifted[at(i), br : 2 * br] = low

    def spread(src, top_ref, low_ref, rows, lead):
        for k in range(lead):
            for c in range(4):
                if lead == 4:
                    tile = src[k // 2, k % 2, c // 2, c % 2]
                else:
                    tile = src[k // 4, k // 2 % 2, k % 2, c // 2, c % 2]
                where = (slice(k * rows, (k + 1) * rows), slice(c * tile.shape[1], (c + 1) * tile.shape[1]))
                top, low = halves(tile)
                top_ref[where] = top
                low_ref[where] = low

    def place(l, value):
        xg[l, 0, z0, y] = value[:, :half]
        xg[l, 1, z0, y] = value[:, half:]

    def give(l, value):
        place(l, value)
        box, other_box = xg.at[l, 0, z0, y], xg.at[l, 1, z0, y]
        first = ship([(box, box, to_y)])
        other = ship([(other_box, other_box, to_z0)])
        return first, other, ship([(box, box, to_z0), (other_box, other_box, to_y)])

    def give_more(l, sent):
        arrived(sent[0])
        box = xg.at[l, 0, z0, 1 - y]
        last = more(sent[2], [(box, box, to_z0)])
        arrived(sent[1])
        box = xg.at[l, 1, 1 - z0, y]
        return more(last, [(box, box, to_y)])

    def give_all(l, value):
        place(l, value)
        box = xg.at[l, :, z0, y]
        return ship([(box, box, target) for target in (to_yz, to_y, to_z0)])

    def against(top_ref, low_ref, l):
        result = None
        for h in range(2):
            top, low = halves(xg[l, h].reshape(n, half))
            lanes = slice(h * half, (h + 1) * half)
            left = jnp.concatenate([top_ref[:, lanes], low_ref[:, lanes]], 0)
            both = mm(left, top, NT)
            term = both[: 2 * br] + both[2 * br :] + mm(top_ref[:, lanes], low, NT)
            result = term if result is None else result + term
        return result

    def make_u():
        tile = pl.ds(pl.multiple_of((2 * z0 + y) * r1, r1), r1)
        u_top[0:br, :], u_low[0:br, :] = halves(tall3(e_top[at(0), :], e_low[at(0), :], d1_top[...], d1_low[...], NT))
        u_top[br : 2 * br, :] = d1_top[:, tile].T
        u_low[br : 2 * br, :] = d1_low[:, tile].T

    def make_v():
        value = tall3(u_top[...], u_low[...], c_top[...], c_low[...], NN)
        v_top[0:br, :], v_low[0:br, :] = halves(cpl[at(1), :] - value[0:br])
        v_top[br : 2 * br, :], v_low[br : 2 * br, :] = halves(-value[br : 2 * br])

    begin_forward()
    land(*got_own)
    pl.semaphore_wait(barrier, len(partners))
    d1_s = first_wave(d1b, order_1)
    c_s = first_wave(cb, order_c)
    forward_step(0)
    forward_step(1)
    forward_step(2)
    forward_step(3)
    forward_step(4)
    forward_step(5)
    d2_z = ship([(sinv.at[pl.ds(r1, r2)], d2b.at[z1, z0, y, x, core], to_z1)])
    arrived(d1_s[0])
    d1_s = second_wave(d1b, order_1, d1_s)
    forward_step(6)
    end_forward()
    arrived(c_s[0])
    c_s = second_wave(cb, order_c, c_s)
    make_part(0)
    a1 = send_part(0)
    make_part(1)
    arrived(d1_s[0])
    d1_l = third_wave(d1b, order_1, d1_s)
    d1_d = cross(d1b, order_1, False)
    b1 = second(0, a1)
    backward_step(6)
    arrived(d2_z)
    d2_s = first_wave(d2b, order_2, lead=every)
    a2 = send_part(1)
    backward_step(5)
    arrived(c_s[0])
    c_l = third_wave(cb, order_c, c_s)
    c_d = cross(cb, order_c, False)
    backward_step(4)
    arrived(d1_l)
    d1_e = cross(d1b, order_1, True)
    arrived(d2_s[0])
    d2_s = second_wave(d2b, order_2, d2_s, lead=every)
    arrived(d1_d)
    arrived(d1_e)
    spread(d1b, d1_top, d1_low, r1, 4)
    b2 = second(1, a2)
    s_1 = total(0, b1)
    z_1 = tall(s_1, d1_top[...], d1_low[...], NT)
    arrived(c_l)
    c_e = cross(cb, order_c, True)
    arrived(c_d)
    arrived(c_e)
    spread(cb, c_top, c_low, r1, 4)
    make_u()
    g1 = give(0, z_1)
    arrived(d2_s[0])
    d2_l = third_wave(d2b, order_2, d2_s, lead=every)
    s_2 = total(1, b2)
    tsend[...] = s_2 - tall(z_1, c_top[...], c_low[...])
    ts = ship([(tsend, trecv, to_z1)])
    backward_step(3)
    make_v()
    d2_d = cross(d2b, order_2, False, lead=every)
    g1 = give_more(0, g1)
    backward_step(2)
    backward_step(1)
    arrived(d2_l)
    d2_e = cross(d2b, order_2, True, lead=every)
    arrived(d2_d)
    arrived(d2_e)
    spread(d2b, d2_top, d2_low, r2, 8)
    arrived(ts)
    z_2 = tall(tsend[...] + trecv[...], d2_top[...], d2_low[...], NT)
    x_2 = tall(z_2, d2_top[...], d2_low[...])
    g2 = give_all(1, x_2)
    arrived(g1)
    base = against(u_top, u_low, 0)
    backward_step(0)
    arrived(g2)
    base = base + against(v_top, v_low, 1)
    top, low = halves(base[0:br])
    fixed[...] = jnp.concatenate([top, low], 1)
    sout[0:r1, :] = base[br : 2 * br]
    tmp[...] = xg[1, z1, :, :, :, pl.ds(pl.multiple_of(z0 * 2 * r2, 2 * r2), 2 * r2)].reshape(n, 2 * r2).T
    sout[r1 : r1 + r2, :] = tmp[pl.ds(pl.multiple_of(y * r2, r2), r2), :]
    land(send.at[0], sum(shipped))


def fused(leaf_rhs, leaf_inverse, leaf_blocks, leaf_pattern, leaf_coupling, sep_rhs, sep_inverse, sep_coupling):
    rows, n = leaf_rhs.shape
    br = leaf_inverse.shape[1]
    sep = leaf_coupling.shape[1]
    half, w = sep // 2, n // 4
    r1, r2 = sep // 4, sep // 8
    tile = sep_inverse.shape[1]
    vm = pl.BlockSpec(memory_space=pltpu.VMEM)
    V = pltpu.VMEM
    solved, lifted, fixed, sout = pl.pallas_call(
        whole_kernel,
        out_shape=(
            pltpu.VMEM((rows, n), F32),
            pltpu.VMEM((rows, 2 * br), BF16),
            pltpu.VMEM((br, 2 * n), BF16),
            pltpu.VMEM(sep_rhs.shape, F32),
        ),
        in_specs=[pl.BlockSpec(memory_space=pltpu.HBM)] * 8,
        out_specs=(vm, vm, vm, vm),
        scratch_shapes=[
            V(leaf_rhs.shape, F32), V(leaf_inverse.shape, F32), V(leaf_blocks.shape, F32),
            pltpu.SMEM(leaf_pattern.shape, jnp.int32),
            V(leaf_coupling.shape, F32), V(sep_rhs.shape, F32),
            V((rows, rows), BF16), V((rows, rows), BF16),
            V((n + br, rows), BF16), V((n + br, rows), BF16),
            V(leaf_coupling.shape, BF16), V(leaf_coupling.shape, BF16),
            V((2, 2, 2, 2, r1, tile), F32),
            V((2, 2, 2, 2, r1, tile), F32),
            V((2, 2, 2, 2, 2, r2, tile), F32),
            V((sep, sep), BF16), V((sep, sep), BF16),
            V((sep, sep), BF16), V((sep, sep), BF16),
            V((sep, sep), BF16), V((sep, sep), BF16),
            V((sep, n), F32),
            V((2, 2, 2, 2, w, half), F32),
            V((2, 2, 2, w, half), F32),
            V((2, 2, w, half), F32),
            V((2, 2, w, half), F32),
            V((w, sep), F32), V((w, sep), F32),
            V((2, 2, 2, 2, w, half), F32),
            V((2 * r2, n), F32),
            V((2 * br, sep), BF16), V((2 * br, sep), BF16),
            V((2 * br, sep), BF16), V((2 * br, sep), BF16),
            V((12 * 1024, 128), F32),
            pltpu.SemaphoreType.DMA((1,)),
            pltpu.SemaphoreType.DMA((27,)),
            pltpu.SemaphoreType.DMA((6,)),
        ],
        compiler_params=pltpu.CompilerParams(
            collective_id=0, has_side_effects=True, vmem_limit_bytes=65_800_000
        ),
    )(leaf_rhs, leaf_inverse, leaf_blocks, leaf_pattern, leaf_coupling, sep_rhs, sep_inverse, sep_coupling)

    return pl.pallas_call(
        finish_kernel,
        out_shape=(
            jax.ShapeDtypeStruct((rows, n), F32),
            jax.ShapeDtypeStruct(sep_rhs.shape, F32),
        ),
        in_specs=[vm] * 4,
        out_specs=[pl.BlockSpec(memory_space=pl.ANY)] * 2,
        scratch_shapes=[V((rows, n), F32), pltpu.SemaphoreType.DMA((2,))],
        compiler_params=pltpu.CompilerParams(vmem_limit_bytes=8 * 1024 * 1024),
    )(solved, lifted, fixed, sout)


def finish_kernel(solved, lifted, fixed, sout, out_far, sout_far, out, near):
    br = fixed.shape[0]
    sep_copy = pltpu.make_async_copy(sout, sout_far, near.at[0])
    sep_copy.start()
    both = fixed[...]
    for i in range(solved.shape[0] // br):
        rows = slice(i * br, (i + 1) * br)
        out[rows, :] = solved[rows, :] - wide(lifted[rows, 0:br], lifted[rows, br : 2 * br], both)
        pltpu.make_async_copy(out.at[pl.ds(i * br, br)], out_far.at[pl.ds(i * br, br)], near.at[1]).start()
    sep_copy.wait()
    pltpu.make_async_copy(out, out_far, near.at[1]).wait()


def pick(*args):
    leaf_rhs, leaf_inverse, _, _, leaf_coupling, _, sep_inverse, _ = args
    if (
        lax.axis_size("leaf") == 8
        and lax.axis_size("col") == 4
        and leaf_inverse.shape[1] == leaf_rhs.shape[1] == sep_inverse.shape[1]
        and leaf_coupling.shape[1] == 4 * sep_inverse.shape[1]
    ):
        return fused(*args)
    return shards(*args)


def solution(mesh):
    return jax.shard_map(
        pick,
        mesh=mesh,
        in_specs=(
            P("leaf", "col"),
            P("leaf", None, None),
            P("leaf", None, None),
            P("leaf", None),
            P("leaf", None),
            P("leaf", "col"),
            P("leaf", "col"),
            P("leaf", "col"),
        ),
        out_specs=(P("leaf", "col"), P("leaf", "col")),
        check_vma=False,
    )
```

```python
import functools

import jax
import jax.numpy as jnp
from jax import lax
from jax.experimental import pallas as pl
from jax.experimental.pallas import tpu as pltpu
from jax.sharding import PartitionSpec as P

HIGH = lax.Precision.HIGHEST
F32 = jnp.float32
BF16 = jnp.bfloat16
NN = ((1,), (0,))
NT = ((1,), (1,))


def from_partner(shard, axis, apart):
    return lax.ppermute(shard, axis, [(i, i ^ 1 << apart) for i in range(lax.axis_size(axis))])


def product(left_side, right_side):
    return jnp.dot(left_side, right_side, precision=HIGH, preferred_element_type=jnp.float32)


def product_first(left_side, right_side):
    return lax.dot_general(
        left_side,
        right_side,
        (((0,), (0,)), ((), ())),
        precision=HIGH,
        preferred_element_type=jnp.float32,
    )


def group_sizes(leaf_count):
    result = []
    for level_index in range(1, 5):
        group_span = 4**level_index
        if group_span // 4 < leaf_count:
            result.append(min(group_span, leaf_count))
    return result


def group_total(partial_value, group_size):
    bit_count = group_size.bit_length() - 1
    for bit_place in range(bit_count):
        partial_value = partial_value + from_partner(partial_value, "leaf", bit_place)
    return partial_value


def shards(
    leaf_rhs,
    leaf_inverse,
    leaf_blocks,
    leaf_pattern,
    leaf_coupling,
    sep_rhs,
    sep_inverse,
    sep_coupling,
):
    inverse_full, coupling_full = (
        lax.all_gather(sep_inverse, "col", axis=1, tiled=True),
        lax.all_gather(sep_coupling, "col", axis=1, tiled=True),
    )
    leaf_count = lax.axis_size("leaf")
    position = lax.axis_index("leaf")
    block_count = leaf_inverse.shape[0]
    block_rows = leaf_inverse.shape[1]
    columns = leaf_rhs.shape[1]
    sep_rows = inverse_full.shape[1]
    weighted = leaf_blocks * leaf_pattern[0].astype(jnp.float32)[:, None, None]
    rhs_blocks = leaf_rhs.reshape(block_count, block_rows, columns)
    column_starts = []
    running = 0
    for column_index in range(block_count):
        column_starts.append(running)
        running = running + block_count - 1 - column_index
    pending = [rhs_blocks[i] for i in range(block_count)]
    forward = []
    for column_index in range(block_count):
        solved = product(leaf_inverse[column_index], pending[column_index])
        forward.append(solved)
        below_count = block_count - 1 - column_index
        if below_count:
            pair_start = column_starts[column_index]
            column_blocks = weighted[pair_start : pair_start + below_count].reshape(
                below_count * block_rows, block_rows
            )
            update = product(column_blocks, solved).reshape(below_count, block_rows, columns)
            for later_index in range(below_count):
                pending[column_index + 1 + later_index] = (
                    pending[column_index + 1 + later_index] - update[later_index]
                )
    sizes_list = group_sizes(leaf_count)
    level_total = len(sizes_list)
    row_counts = [sep_rows // size_item for size_item in sizes_list]
    offsets = []
    running = 0
    for row_count in row_counts:
        offsets.append(running)
        running = running + row_count
    last_block = forward[-1]
    level_pieces = []
    for level_index in range(level_total):
        group_size = sizes_list[level_index]
        row_count = row_counts[level_index]
        row_offset = offsets[level_index]
        row_start = position % group_size * row_count
        coupling_rows = leaf_coupling[level_index * block_rows : (level_index + 1) * block_rows]
        partial_value = -product_first(coupling_rows, last_block)
        if level_index > 0:
            child_offset = offsets[level_index - 1]
            child_count = row_counts[level_index - 1]
            partial_value = partial_value - product_first(
                coupling_full[child_offset : child_offset + child_count], level_pieces[-1]
            )
        own_rows = (
            lax.dynamic_slice_in_dim(partial_value, row_start, row_count, 0)
            + sep_rhs[row_offset : row_offset + row_count]
        )
        partial_value = lax.dynamic_update_slice_in_dim(partial_value, own_rows, row_start, 0)
        summed = group_total(partial_value, group_size)
        level_pieces.append(product(inverse_full[row_offset : row_offset + row_count], summed))
    correction = jnp.zeros((block_rows, columns), jnp.float32)
    solution_pieces = [None] * level_total
    parent_full = None
    for level_index in reversed(range(level_total)):
        group_size = sizes_list[level_index]
        row_count = row_counts[level_index]
        row_offset = offsets[level_index]
        row_start = position % group_size * row_count
        target = level_pieces[level_index]
        if parent_full is not None:
            target = target - product(
                coupling_full[row_offset : row_offset + row_count], parent_full
            )
        partial_value = product_first(inverse_full[row_offset : row_offset + row_count], target)
        parent_full = group_total(partial_value, group_size)
        solution_pieces[level_index] = lax.dynamic_slice_in_dim(
            parent_full, row_start, row_count, 0
        )
        correction = correction + product(
            leaf_coupling[level_index * block_rows : (level_index + 1) * block_rows], parent_full
        )
    pending = list(forward)
    pending[-1] = pending[-1] - correction
    backward = [None] * block_count
    for column_index in reversed(range(block_count)):
        target = pending[column_index]
        below_count = block_count - 1 - column_index
        if below_count:
            pair_start = column_starts[column_index]
            column_blocks = weighted[pair_start : pair_start + below_count].reshape(
                below_count * block_rows, block_rows
            )
            later_blocks = jnp.concatenate(backward[column_index + 1 :], 0)
            target = target - product_first(column_blocks, later_blocks)
        backward[column_index] = product_first(leaf_inverse[column_index], target)
    return (jnp.concatenate(backward, 0), jnp.concatenate(solution_pieces, 0))


def halves(value):
    top = value.astype(BF16)
    return top, (value - top.astype(F32)).astype(BF16)


def mm(left_side, right_side, dims=NN):
    return lax.dot_general(
        left_side, right_side, (dims, ((), ())), preferred_element_type=F32
    )


def wide(left_top, left_low, right_both):
    n = right_both.shape[1] // 2
    both = mm(left_top, right_both)
    return both[:, :n] + both[:, n:] + mm(left_low, right_both[:, :n])


def tall(left_side, right_top, right_low, dims=NN):
    n = left_side.shape[0]
    top, low = halves(left_side)
    both = mm(jnp.concatenate([top, low], 0), right_top, dims)
    return both[:n] + both[n:] + mm(top, right_low, dims)


def tall3(left_top, left_low, right_top, right_low, dims=NN):
    n = left_top.shape[0]
    both = mm(jnp.concatenate([left_top, left_low], 0), right_top, dims)
    return both[:n] + both[n:] + mm(left_top, right_low, dims)


def whole_kernel(
    rhs_far, inv_far, blk_far, pat_far, cpl_far, srhs_far, sinv, scpl,
    solved, lifted, fixed, sout,
    rhs, inv, blk, pat, cpl, srhs,
    l_top, l_low, xt_top, xt_low,
    e_top, e_low, d1b, cb, d2b, d1_top, d1_low, c_top, c_low, d2_top, d2_low,
    pad, part, ra, acc, rb, tsend, trecv, xg, tmp, u_top, u_low, v_top, v_low, q_top, q_low, r_top, r_low, gauge, send, recv, near,
):
    leaf = lax.axis_index("leaf")
    col = lax.axis_index("col")
    y = lax.rem(leaf, 2)
    z0 = lax.rem(lax.div(leaf, 2), 2)
    z1 = lax.div(leaf, 4)
    core = lax.rem(col, 2)
    x = lax.div(col, 2)
    to_core = (leaf, col + 1 - 2 * core)
    to_z1 = (leaf + 4 - 8 * z1, col)

    def across(names):
        target_leaf, target_col = leaf, col
        if "y" in names:
            target_leaf = target_leaf + 1 - 2 * y
        if "z" in names:
            target_leaf = target_leaf + 2 - 4 * z0
        if "x" in names:
            target_col = target_col + 2 - 4 * x
        return target_leaf, target_col

    to_y, to_z0, to_yz = across("y"), across("z"), across("yz")
    barrier = pltpu.get_barrier_semaphore()
    partners = (to_core, to_z1) + tuple(across(names) for names in ('x', 'y', 'yz', 'z'))
    for partner in partners:
        pl.semaphore_signal(
            barrier, inc=1, device_id=partner, device_id_type=pl.DeviceIdType.MESH
        )
    nb, br = inv.shape[0], inv.shape[1]
    n = rhs.shape[1]
    sep = cpl.shape[1]
    half = sep // 2
    r1, r2 = sep // 4, sep // 8
    w = n // 4
    starts = []
    running = 0
    for j in range(nb):
        starts.append(running)
        running += nb - 1 - j

    def rows_of(ref):
        count = 1
        for size in ref.shape:
            count *= size
        return count // 128

    def land(semaphore, count):
        box = gauge.at[pl.ds(0, count)]
        pltpu.make_async_copy(box, box, semaphore).wait()

    loads = []

    def fetch(*pairs):
        semaphore = near.at[len(loads)]
        loads.append(semaphore)
        count = 0
        for src, dst in pairs:
            pltpu.make_async_copy(src, dst, semaphore).start()
            count += rows_of(dst)
        return semaphore, count

    pat_copy = pltpu.make_async_copy(pat_far, pat, near.at[0])
    pat_copy.start()
    loads.append(near.at[0])
    got_own = fetch(
        (sinv.at[pl.ds(0, r1)], d1b.at[z0, y, x, core]),
        (scpl, cb.at[z0, y, x, core]),
        (sinv.at[pl.ds(r1, r2)], d2b.at[z1, z0, y, x, core]),
    )
    got_main = fetch((inv_far, inv), (rhs_far, rhs))
    got_blk = []
    for begin, end in ((0, starts[1]), (starts[1], running)):
        box = pl.ds(begin, end - begin)
        got_blk.append(fetch((blk_far.at[box], blk.at[box])))
    got_rest = fetch((cpl_far, cpl), (srhs_far, srhs))

    shipped = []
    groups = []

    def begin_moves(semaphore, moves):
        count = 0
        for src, dst, target in moves:
            pltpu.make_async_remote_copy(
                src_ref=src, dst_ref=dst, send_sem=send.at[0], recv_sem=semaphore,
                device_id=target, device_id_type=pl.DeviceIdType.MESH,
            ).start()
            count += rows_of(dst)
        shipped.append(count)
        return count

    def ship(moves):
        semaphore = recv.at[len(groups)]
        groups.append(len(moves))
        return semaphore, begin_moves(semaphore, moves)

    def more(sent, moves):
        return sent[0], sent[1] + begin_moves(sent[0], moves)

    def arrived(sent):
        land(*sent)

    partner_of = {name: across(name) for name in "xyz"}
    place_of = {"x": x, "y": y, "z": z0}
    order_1 = (("yzx", 3), ("zyx", 3), ("xyz", 1), ("xzy", 1))
    order_c = (("yzx", 5), ("zyx", 5), ("xyz", 3), ("xzy", 3))
    order_2 = (("yzx", 5), ("zyx", 5), ("xyz", 3), ("xzy", 3))
    every = (slice(None),)

    def row_parts(count, orders):
        units = count // 8
        weight = sum(share for _, share in orders)
        result = []
        begin = seen = 0
        for order, share in orders:
            seen += share
            end = seen * units // weight * 8
            result.append((order, begin, end - begin))
            begin = end
        return result

    def tile(ref, lead, begin, size, far):
        where = tuple(1 - place_of[name] if name in far else place_of[name] for name in "zyx")
        return ref.at[lead + where + (core, pl.ds(begin, size))]

    def first_wave(ref, orders, lead=()):
        near_moves, last_moves = [], []
        parts = row_parts(ref.shape[-2], orders)
        for k in range(3):
            for order, begin, size in parts:
                box = tile(ref, lead, begin, size, "")
                move = (box, box, partner_of[order[k]])
                (last_moves if k == 2 else near_moves).append(move)
        started = ship(near_moves)
        last = ship(last_moves)
        return started, last

    def second_wave(ref, orders, sent, short, lead=()):
        near_moves, last_moves = [], []
        for order, begin, size in row_parts(ref.shape[-2], orders):
            p, q, r = order
            box = tile(ref, lead, begin, size, p)
            if short:
                near_moves.append((box, box, across(q + r)))
            near_moves.append((box, box, partner_of[q]))
            last_moves.append((box, box, partner_of[r]))
            box = tile(ref, lead, begin, size, q)
            last_moves.append((box, box, partner_of[r]))
        if short:
            return None, more(sent[1], near_moves + last_moves)
        started = ship(near_moves)
        return started, more(sent[1], last_moves)

    def third_wave(ref, orders, sent, lead=()):
        moves = []
        for order, begin, size in row_parts(ref.shape[-2], orders):
            box = tile(ref, lead, begin, size, order[:2])
            moves.append((box, box, partner_of[order[2]]))
        return more(sent[1], moves)

    def cross(ref, orders, fresh, lead=()):
        moves = []
        for order, begin, size in row_parts(ref.shape[-2], orders):
            where = []
            for name in "zyx":
                if name != order[2]:
                    where.append(slice(None))
                else:
                    where.append(1 - place_of[name] if fresh else place_of[name])
            box = ref.at[lead + tuple(where) + (core, pl.ds(begin, size))]
            moves.append((box, box, to_core))
        return ship(moves)

    def at(i):
        return slice(i * br, (i + 1) * br)

    def load_column(j):
        if j < 2:
            land(*got_blk[j])
        l_top[at(j), at(j)], l_low[at(j), at(j)] = halves(inv[j])
        for i in range(j + 1, nb):
            p = starts[j] + i - j - 1
            block = blk[p] * pat[0, p].astype(F32)
            l_top[at(i), at(j)], l_low[at(i), at(j)] = halves(block)

    pending = []
    forward = [None] * nb

    def begin_forward():
        pat_copy.wait()
        land(*got_main)
        pending.extend(rhs[at(i)] for i in range(nb))

    def forward_step(j):
        load_column(j)
        top, low = halves(pending[j])
        solved_j = wide(l_top[at(j), at(j)], l_low[at(j), at(j)], jnp.concatenate([top, low], 1))
        forward[j] = solved_j
        top, low = halves(solved_j)
        both = jnp.concatenate([top, low], 1)
        for i in range(j + 1, nb):
            pending[i] = pending[i] - wide(l_top[at(i), at(j)], l_low[at(i), at(j)], both)

    last_t = []

    def end_forward():
        land(*got_rest)
        e_top[...], e_low[...] = halves(cpl[...])
        last_t.append(forward[nb - 1].T)

    def make_part(l):
        pad[...] = jnp.zeros_like(pad)
        if l == 0:
            pad[pl.ds(pl.multiple_of((2 * z0 + y) * r1, r1), r1), :] = srhs[0:r1]
        else:
            pad[pl.ds(pl.multiple_of(leaf * r2, r2), r2), :] = srhs[r1 : r1 + r2]
        term = pad[...].T - tall(last_t[0], e_top[at(l), :], e_low[at(l), :])
        for h in range(2):
            part[l, h] = term[:, h * half : (h + 1) * half].reshape(2, 2, w, half)

    def send_part(l, short):
        if short:
            return ship([
                (part.at[l, :, 1 - z0, 1 - y], ra.at[l, 0], to_yz),
                (part.at[l, :, z0, 1 - y], ra.at[l, 1], to_y),
                (part.at[l, :, 1 - z0, y], ra.at[l, 2], to_z0),
            ])
        first = ship([(part.at[l, 0, 1 - z0, 1 - y], ra.at[l, 0, 0], to_y)])
        other = ship([(part.at[l, 1, 1 - z0, 1 - y], ra.at[l, 1, 0], to_z0)])
        last = ship([
            (part.at[l, 0, z0, 1 - y], ra.at[l, 0, 1], to_y),
            (part.at[l, 1, 1 - z0, y], ra.at[l, 1, 1], to_z0),
        ])
        return first, other, last

    def second(l, sent):
        arrived(sent[0])
        acc[l, 0] = part[l, 0, 1 - z0, y] + ra[l, 0, 0]
        last = more(sent[2], [(acc.at[l, 0], rb.at[l, 0], to_z0)])
        arrived(sent[1])
        acc[l, 1] = part[l, 1, z0, 1 - y] + ra[l, 1, 0]
        return more(last, [(acc.at[l, 1], rb.at[l, 1], to_y)])

    def total(l, sent, short):
        arrived(sent)
        if short:
            return jnp.concatenate(
                [part[l, h, z0, y] + ra[l, 0, h] + (ra[l, 1, h] + ra[l, 2, h]) for h in range(2)], 1
            )
        return jnp.concatenate([part[l, h, z0, y] + ra[l, h, 1] + rb[l, h] for h in range(2)], 1)

    row = lax.broadcasted_iota(jnp.int32, (br, br), 0)
    column = lax.broadcasted_iota(jnp.int32, (br, br), 1)
    unit = jnp.where(row == column, 1.0, 0.0).astype(F32)

    def backward_step(i):
        first = forward[i].T
        below = unit if i == nb - 1 else jnp.zeros((br, br), F32)
        target = jnp.concatenate([first, below], 0)
        if i < nb - 1:
            rest = slice((i + 1) * br, nb * br)
            target = target - (
                mm(xt_top[:, rest], l_top[rest, at(i)])
                + mm(xt_low[:, rest], l_top[rest, at(i)])
                + mm(xt_top[:, rest], l_low[rest, at(i)])
            )
        value = tall(target, l_top[at(i), at(i)], l_low[at(i), at(i)])
        xt_top[:, at(i)], xt_low[:, at(i)] = halves(value)
        solved[at(i), :] = value[:n].T
        top, low = halves(value[n:].T)
        lifted[at(i), 0:br] = top
        lifted[at(i), br : 2 * br] = low

    def spread(src, top_ref, low_ref, rows, lead):
        for k in range(lead):
            for c in range(4):
                if lead == 4:
                    tile = src[k // 2, k % 2, c // 2, c % 2]
                else:
                    tile = src[k // 4, k // 2 % 2, k % 2, c // 2, c % 2]
                where = (slice(k * rows, (k + 1) * rows), slice(c * tile.shape[1], (c + 1) * tile.shape[1]))
                top, low = halves(tile)
                top_ref[where] = top
                low_ref[where] = low

    def place(l, value):
        xg[l, 0, z0, y] = value[:, :half]
        xg[l, 1, z0, y] = value[:, half:]

    def give(l, value):
        place(l, value)
        box, other_box = xg.at[l, 0, z0, y], xg.at[l, 1, z0, y]
        first = ship([(box, box, to_y)])
        other = ship([(other_box, other_box, to_z0)])
        return first, other, ship([(box, box, to_z0), (other_box, other_box, to_y)])

    def give_more(l, sent):
        arrived(sent[0])
        box = xg.at[l, 0, z0, 1 - y]
        last = more(sent[2], [(box, box, to_z0)])
        arrived(sent[1])
        box = xg.at[l, 1, 1 - z0, y]
        return more(last, [(box, box, to_y)])

    def give_all(l, value):
        place(l, value)
        box = xg.at[l, :, z0, y]
        return ship([(box, box, target) for target in (to_yz, to_y, to_z0)])

    def against(top_ref, low_ref, l):
        result = None
        for h in range(2):
            top, low = halves(xg[l, h].reshape(n, half))
            lanes = slice(h * half, (h + 1) * half)
            both = mm(top_ref[:, lanes], jnp.concatenate([top, low], 0), NT)
            term = both[:, :n] + both[:, n:] + mm(low_ref[:, lanes], top, NT)
            result = term if result is None else result + term
        return result

    def make_u():
        tile = pl.ds(pl.multiple_of((2 * z0 + y) * r1, r1), r1)
        u_top[0:br, :], u_low[0:br, :] = halves(tall3(e_top[at(0), :], e_low[at(0), :], d1_top[...], d1_low[...], NT))
        u_top[br : 2 * br, :] = d1_top[:, tile].T
        u_low[br : 2 * br, :] = d1_low[:, tile].T

    def make_v():
        value = tall3(u_top[...], u_low[...], c_top[...], c_low[...], NN)
        v_top[0:br, :], v_low[0:br, :] = halves(cpl[at(1), :] - value[0:br])
        v_top[br : 2 * br, :], v_low[br : 2 * br, :] = halves(-value[br : 2 * br])

    def make_q():
        pair = pl.ds(pl.multiple_of((2 * z1 + z0) * 2 * r2, 2 * r2), 2 * r2)
        q_top[0 : 2 * br, :], q_low[0 : 2 * br, :] = halves(
            tall3(v_top[...], v_low[...], d2_top[...], d2_low[...], NT)
        )
        q_top[2 * br :, :] = d2_top[:, pair].T
        q_low[2 * br :, :] = d2_low[:, pair].T

    def make_r():
        r_top[...], r_low[...] = halves(tall3(q_top[...], q_low[...], d2_top[...], d2_low[...], NN))

    def rows_part(c):
        return pl.ds(c * (w // 2), w // 2)

    def give_part(l, c, sent):
        rows = rows_part(c)
        value = tsend[rows, :] + trecv[rows, :]
        xg[l, 0, z0, y, rows] = value[:, :half]
        xg[l, 1, z0, y, rows] = value[:, half:]
        box = xg.at[l, :, z0, y, rows]
        moves = [(box, box, target) for target in (to_yz, to_y, to_z0)]
        return ship(moves) if sent is None else more(sent, moves)

    begin_forward()
    land(*got_own)
    pl.semaphore_wait(barrier, len(partners))
    d1_s = first_wave(d1b, order_1)
    forward_step(0)
    forward_step(1)
    c_s = first_wave(cb, order_c)
    forward_step(2)
    forward_step(3)
    forward_step(4)
    d2_z = ship([(sinv.at[pl.ds(r1, r2)], d2b.at[z1, z0, y, x, core], to_z1)])
    arrived(d1_s[0])
    d1_s = second_wave(d1b, order_1, d1_s, False)
    forward_step(5)
    forward_step(6)
    end_forward()
    arrived(c_s[0])
    c_s = second_wave(cb, order_c, c_s, False)
    make_part(0)
    a1 = send_part(0, False)
    make_part(1)
    a2 = send_part(1, False)
    arrived(d1_s[0])
    d1_l = third_wave(d1b, order_1, d1_s)
    b1 = second(0, a1)
    arrived(c_s[0])
    c_l = third_wave(cb, order_c, c_s)
    backward_step(6)
    d1_d = cross(d1b, order_1, False)
    arrived(d2_z)
    d2_s = first_wave(d2b, order_2, lead=every)
    backward_step(5)
    c_d = cross(cb, order_c, False)
    backward_step(4)
    arrived(d1_l)
    d1_e = cross(d1b, order_1, True)
    arrived(d1_d)
    arrived(d1_e)
    spread(d1b, d1_top, d1_low, r1, 4)
    b2 = second(1, a2)
    arrived(c_l)
    c_e = cross(cb, order_c, True)
    arrived(d2_s[0])
    d2_s = second_wave(d2b, order_2, d2_s, False, lead=every)
    s_1 = total(0, b1, False)
    z_1 = tall(s_1, d1_top[...], d1_low[...], NT)
    arrived(c_d)
    arrived(c_e)
    spread(cb, c_top, c_low, r1, 4)
    make_u()
    g1 = give(0, z_1)
    s_2 = total(1, b2, False)
    tsend[...] = s_2 - tall(z_1, c_top[...], c_low[...])
    ts = [ship([(tsend.at[rows_part(c)], trecv.at[rows_part(c)], to_z1)]) for c in range(2)]
    arrived(d2_s[0])
    d2_l = third_wave(d2b, order_2, d2_s, lead=every)
    backward_step(3)
    make_v()
    g1 = give_more(0, g1)
    d2_d = cross(d2b, order_2, False, lead=every)
    backward_step(2)
    backward_step(1)
    arrived(ts[0])
    g2 = give_part(1, 0, None)
    arrived(d2_l)
    d2_e = cross(d2b, order_2, True, lead=every)
    arrived(ts[1])
    g2 = give_part(1, 1, g2)
    arrived(d2_d)
    arrived(d2_e)
    spread(d2b, d2_top, d2_low, r2, 8)
    make_q()
    make_r()
    arrived(g1)
    base = against(u_top, u_low, 0)
    backward_step(0)
    arrived(g2)
    rest = against(r_top, r_low, 1)
    top, low = halves(base[0:br] + rest[0:br])
    fixed[...] = jnp.concatenate([top, low], 1)
    sout[0:r1, :] = base[br : 2 * br] + rest[br : 2 * br]
    tmp[...] = rest[2 * br :]
    sout[r1 : r1 + r2, :] = tmp[pl.ds(pl.multiple_of(y * r2, r2), r2), :]
    land(send.at[0], sum(shipped))


def fused(leaf_rhs, leaf_inverse, leaf_blocks, leaf_pattern, leaf_coupling, sep_rhs, sep_inverse, sep_coupling):
    rows, n = leaf_rhs.shape
    br = leaf_inverse.shape[1]
    sep = leaf_coupling.shape[1]
    half, w = sep // 2, n // 4
    r1, r2 = sep // 4, sep // 8
    tile = sep_inverse.shape[1]
    vm = pl.BlockSpec(memory_space=pltpu.VMEM)
    V = pltpu.VMEM
    solved, lifted, fixed, sout = pl.pallas_call(
        whole_kernel,
        out_shape=(
            pltpu.VMEM((rows, n), F32),
            pltpu.VMEM((rows, 2 * br), BF16),
            pltpu.VMEM((br, 2 * n), BF16),
            pltpu.VMEM(sep_rhs.shape, F32),
        ),
        in_specs=[pl.BlockSpec(memory_space=pltpu.HBM)] * 8,
        out_specs=(vm, vm, vm, vm),
        scratch_shapes=[
            V(leaf_rhs.shape, F32), V(leaf_inverse.shape, F32), V(leaf_blocks.shape, F32),
            pltpu.SMEM(leaf_pattern.shape, jnp.int32),
            V(leaf_coupling.shape, F32), V(sep_rhs.shape, F32),
            V((rows, rows), BF16), V((rows, rows), BF16),
            V((n + br, rows), BF16), V((n + br, rows), BF16),
            V(leaf_coupling.shape, BF16), V(leaf_coupling.shape, BF16),
            V((2, 2, 2, 2, r1, tile), F32),
            V((2, 2, 2, 2, r1, tile), F32),
            V((2, 2, 2, 2, 2, r2, tile), F32),
            V((sep, sep), BF16), V((sep, sep), BF16),
            V((sep, sep), BF16), V((sep, sep), BF16),
            V((sep, sep), BF16), V((sep, sep), BF16),
            V((sep, n), F32),
            V((2, 2, 2, 2, w, half), F32),
            V((2, 3, 2, w, half), F32),
            V((2, 2, w, half), F32),
            V((2, 2, w, half), F32),
            V((w, sep), F32), V((w, sep), F32),
            V((2, 2, 2, 2, w, half), F32),
            V((2 * r2, n), F32),
            V((2 * br, sep), BF16), V((2 * br, sep), BF16),
            V((2 * br, sep), BF16), V((2 * br, sep), BF16),
            V((2 * br + 2 * r2, sep), BF16), V((2 * br + 2 * r2, sep), BF16),
            V((2 * br + 2 * r2, sep), BF16), V((2 * br + 2 * r2, sep), BF16),
            V((12 * 1024, 128), F32),
            pltpu.SemaphoreType.DMA((1,)),
            pltpu.SemaphoreType.DMA((28,)),
            pltpu.SemaphoreType.DMA((6,)),
        ],
        compiler_params=pltpu.CompilerParams(
            collective_id=0, has_side_effects=True, vmem_limit_bytes=65_800_000
        ),
    )(leaf_rhs, leaf_inverse, leaf_blocks, leaf_pattern, leaf_coupling, sep_rhs, sep_inverse, sep_coupling)

    return pl.pallas_call(
        finish_kernel,
        out_shape=(
            jax.ShapeDtypeStruct((rows, n), F32),
            jax.ShapeDtypeStruct(sep_rhs.shape, F32),
        ),
        in_specs=[vm] * 4,
        out_specs=[pl.BlockSpec(memory_space=pl.ANY)] * 2,
        scratch_shapes=[V((rows, n), F32), pltpu.SemaphoreType.DMA((2,))],
        compiler_params=pltpu.CompilerParams(vmem_limit_bytes=8 * 1024 * 1024),
    )(solved, lifted, fixed, sout)


def finish_kernel(solved, lifted, fixed, sout, out_far, sout_far, out, near):
    br = fixed.shape[0]
    sep_copy = pltpu.make_async_copy(sout, sout_far, near.at[0])
    sep_copy.start()
    both = fixed[...]
    for i in range(solved.shape[0] // br):
        rows = slice(i * br, (i + 1) * br)
        out[rows, :] = solved[rows, :] - wide(lifted[rows, 0:br], lifted[rows, br : 2 * br], both)
        pltpu.make_async_copy(out.at[pl.ds(i * br, br)], out_far.at[pl.ds(i * br, br)], near.at[1]).start()
    sep_copy.wait()
    pltpu.make_async_copy(out, out_far, near.at[1]).wait()


def pick(*args):
    leaf_rhs, leaf_inverse, _, _, leaf_coupling, _, sep_inverse, _ = args
    if (
        lax.axis_size("leaf") == 8
        and lax.axis_size("col") == 4
        and leaf_inverse.shape[1] == leaf_rhs.shape[1] == sep_inverse.shape[1]
        and leaf_coupling.shape[1] == 4 * sep_inverse.shape[1]
    ):
        return fused(*args)
    return shards(*args)


def solution(mesh):
    return jax.shard_map(
        pick,
        mesh=mesh,
        in_specs=(
            P("leaf", "col"),
            P("leaf", None, None),
            P("leaf", None, None),
            P("leaf", None),
            P("leaf", None),
            P("leaf", "col"),
            P("leaf", "col"),
            P("leaf", "col"),
        ),
        out_specs=(P("leaf", "col"), P("leaf", "col")),
        check_vma=False,
    )
```

```python
import functools

import jax
import jax.numpy as jnp
from jax import lax
from jax.experimental import pallas as pl
from jax.experimental.pallas import tpu as pltpu
from jax.sharding import PartitionSpec as P

HIGH = lax.Precision.HIGHEST
F32 = jnp.float32
BF16 = jnp.bfloat16
NN = ((1,), (0,))
NT = ((1,), (1,))


def from_partner(shard, axis, apart):
    return lax.ppermute(shard, axis, [(i, i ^ 1 << apart) for i in range(lax.axis_size(axis))])


def product(left_side, right_side):
    return jnp.dot(left_side, right_side, precision=HIGH, preferred_element_type=jnp.float32)


def product_first(left_side, right_side):
    return lax.dot_general(
        left_side,
        right_side,
        (((0,), (0,)), ((), ())),
        precision=HIGH,
        preferred_element_type=jnp.float32,
    )


def group_sizes(leaf_count):
    result = []
    for level_index in range(1, 5):
        group_span = 4**level_index
        if group_span // 4 < leaf_count:
            result.append(min(group_span, leaf_count))
    return result


def group_total(partial_value, group_size):
    bit_count = group_size.bit_length() - 1
    for bit_place in range(bit_count):
        partial_value = partial_value + from_partner(partial_value, "leaf", bit_place)
    return partial_value


def shards(
    leaf_rhs,
    leaf_inverse,
    leaf_blocks,
    leaf_pattern,
    leaf_coupling,
    sep_rhs,
    sep_inverse,
    sep_coupling,
):
    inverse_full, coupling_full = (
        lax.all_gather(sep_inverse, "col", axis=1, tiled=True),
        lax.all_gather(sep_coupling, "col", axis=1, tiled=True),
    )
    leaf_count = lax.axis_size("leaf")
    position = lax.axis_index("leaf")
    block_count = leaf_inverse.shape[0]
    block_rows = leaf_inverse.shape[1]
    columns = leaf_rhs.shape[1]
    sep_rows = inverse_full.shape[1]
    weighted = leaf_blocks * leaf_pattern[0].astype(jnp.float32)[:, None, None]
    rhs_blocks = leaf_rhs.reshape(block_count, block_rows, columns)
    column_starts = []
    running = 0
    for column_index in range(block_count):
        column_starts.append(running)
        running = running + block_count - 1 - column_index
    pending = [rhs_blocks[i] for i in range(block_count)]
    forward = []
    for column_index in range(block_count):
        solved = product(leaf_inverse[column_index], pending[column_index])
        forward.append(solved)
        below_count = block_count - 1 - column_index
        if below_count:
            pair_start = column_starts[column_index]
            column_blocks = weighted[pair_start : pair_start + below_count].reshape(
                below_count * block_rows, block_rows
            )
            update = product(column_blocks, solved).reshape(below_count, block_rows, columns)
            for later_index in range(below_count):
                pending[column_index + 1 + later_index] = (
                    pending[column_index + 1 + later_index] - update[later_index]
                )
    sizes_list = group_sizes(leaf_count)
    level_total = len(sizes_list)
    row_counts = [sep_rows // size_item for size_item in sizes_list]
    offsets = []
    running = 0
    for row_count in row_counts:
        offsets.append(running)
        running = running + row_count
    last_block = forward[-1]
    level_pieces = []
    for level_index in range(level_total):
        group_size = sizes_list[level_index]
        row_count = row_counts[level_index]
        row_offset = offsets[level_index]
        row_start = position % group_size * row_count
        coupling_rows = leaf_coupling[level_index * block_rows : (level_index + 1) * block_rows]
        partial_value = -product_first(coupling_rows, last_block)
        if level_index > 0:
            child_offset = offsets[level_index - 1]
            child_count = row_counts[level_index - 1]
            partial_value = partial_value - product_first(
                coupling_full[child_offset : child_offset + child_count], level_pieces[-1]
            )
        own_rows = (
            lax.dynamic_slice_in_dim(partial_value, row_start, row_count, 0)
            + sep_rhs[row_offset : row_offset + row_count]
        )
        partial_value = lax.dynamic_update_slice_in_dim(partial_value, own_rows, row_start, 0)
        summed = group_total(partial_value, group_size)
        level_pieces.append(product(inverse_full[row_offset : row_offset + row_count], summed))
    correction = jnp.zeros((block_rows, columns), jnp.float32)
    solution_pieces = [None] * level_total
    parent_full = None
    for level_index in reversed(range(level_total)):
        group_size = sizes_list[level_index]
        row_count = row_counts[level_index]
        row_offset = offsets[level_index]
        row_start = position % group_size * row_count
        target = level_pieces[level_index]
        if parent_full is not None:
            target = target - product(
                coupling_full[row_offset : row_offset + row_count], parent_full
            )
        partial_value = product_first(inverse_full[row_offset : row_offset + row_count], target)
        parent_full = group_total(partial_value, group_size)
        solution_pieces[level_index] = lax.dynamic_slice_in_dim(
            parent_full, row_start, row_count, 0
        )
        correction = correction + product(
            leaf_coupling[level_index * block_rows : (level_index + 1) * block_rows], parent_full
        )
    pending = list(forward)
    pending[-1] = pending[-1] - correction
    backward = [None] * block_count
    for column_index in reversed(range(block_count)):
        target = pending[column_index]
        below_count = block_count - 1 - column_index
        if below_count:
            pair_start = column_starts[column_index]
            column_blocks = weighted[pair_start : pair_start + below_count].reshape(
                below_count * block_rows, block_rows
            )
            later_blocks = jnp.concatenate(backward[column_index + 1 :], 0)
            target = target - product_first(column_blocks, later_blocks)
        backward[column_index] = product_first(leaf_inverse[column_index], target)
    return (jnp.concatenate(backward, 0), jnp.concatenate(solution_pieces, 0))


def halves(value):
    top = value.astype(BF16)
    return top, (value - top.astype(F32)).astype(BF16)


def mm(left_side, right_side, dims=NN):
    return lax.dot_general(
        left_side, right_side, (dims, ((), ())), preferred_element_type=F32
    )


def wide(left_top, left_low, right_both):
    n = right_both.shape[1] // 2
    both = mm(left_top, right_both)
    return both[:, :n] + both[:, n:] + mm(left_low, right_both[:, :n])


def tall(left_side, right_top, right_low, dims=NN):
    n = left_side.shape[0]
    top, low = halves(left_side)
    both = mm(jnp.concatenate([top, low], 0), right_top, dims)
    return both[:n] + both[n:] + mm(top, right_low, dims)


def tall3(left_top, left_low, right_top, right_low, dims=NN):
    n = left_top.shape[0]
    both = mm(jnp.concatenate([left_top, left_low], 0), right_top, dims)
    return both[:n] + both[n:] + mm(left_top, right_low, dims)


def whole_kernel(
    rhs_far, inv_far, blk_far, pat_far, cpl_far, srhs_far, sinv, scpl,
    solved, lifted, fixed, sout,
    rhs, inv, blk, pat, cpl, srhs,
    l_top, l_low, xt_top, xt_low,
    e_top, e_low, d1b, cb, d2b, d1_top, d1_low, c_top, c_low, d2_top, d2_low,
    pad, part, ra, acc, rb, tsend, trecv, xg, tmp, u_top, u_low, v_top, v_low, q_top, q_low, r_top, r_low, gauge, send, recv, near,
):
    leaf = lax.axis_index("leaf")
    col = lax.axis_index("col")
    y = lax.rem(leaf, 2)
    z0 = lax.rem(lax.div(leaf, 2), 2)
    z1 = lax.div(leaf, 4)
    core = lax.rem(col, 2)
    x = lax.div(col, 2)
    to_core = (leaf, col + 1 - 2 * core)
    to_z1 = (leaf + 4 - 8 * z1, col)

    def across(names):
        target_leaf, target_col = leaf, col
        if "y" in names:
            target_leaf = target_leaf + 1 - 2 * y
        if "z" in names:
            target_leaf = target_leaf + 2 - 4 * z0
        if "x" in names:
            target_col = target_col + 2 - 4 * x
        return target_leaf, target_col

    to_y, to_z0, to_yz = across("y"), across("z"), across("yz")
    barrier = pltpu.get_barrier_semaphore()
    partners = (to_core, to_z1) + tuple(across(names) for names in ('x', 'y', 'yz', 'z'))
    for partner in partners:
        pl.semaphore_signal(
            barrier, inc=1, device_id=partner, device_id_type=pl.DeviceIdType.MESH
        )
    nb, br = inv.shape[0], inv.shape[1]
    n = rhs.shape[1]
    sep = cpl.shape[1]
    half = sep // 2
    r1, r2 = sep // 4, sep // 8
    w = n // 4
    starts = []
    running = 0
    for j in range(nb):
        starts.append(running)
        running += nb - 1 - j

    def rows_of(ref):
        count = 1
        for size in ref.shape:
            count *= size
        return count // 128

    def land(semaphore, count):
        box = gauge.at[pl.ds(0, count)]
        pltpu.make_async_copy(box, box, semaphore).wait()

    loads = []

    def fetch(*pairs):
        semaphore = near.at[len(loads)]
        loads.append(semaphore)
        count = 0
        for src, dst in pairs:
            pltpu.make_async_copy(src, dst, semaphore).start()
            count += rows_of(dst)
        return semaphore, count

    pat_copy = pltpu.make_async_copy(pat_far, pat, near.at[0])
    pat_copy.start()
    loads.append(near.at[0])
    got_own = fetch(
        (sinv.at[pl.ds(0, r1)], d1b.at[z0, y, x, core]),
        (scpl, cb.at[z0, y, x, core]),
        (sinv.at[pl.ds(r1, r2)], d2b.at[z1, z0, y, x, core]),
    )
    got_main = fetch((inv_far, inv), (rhs_far, rhs))
    got_blk = []
    for begin, end in ((0, starts[1]), (starts[1], running)):
        box = pl.ds(begin, end - begin)
        got_blk.append(fetch((blk_far.at[box], blk.at[box])))
    got_rest = fetch((cpl_far, cpl), (srhs_far, srhs))

    shipped = []
    groups = []

    def begin_moves(semaphore, moves):
        count = 0
        for src, dst, target in moves:
            pltpu.make_async_remote_copy(
                src_ref=src, dst_ref=dst, send_sem=send.at[0], recv_sem=semaphore,
                device_id=target, device_id_type=pl.DeviceIdType.MESH,
            ).start()
            count += rows_of(dst)
        shipped.append(count)
        return count

    def ship(moves):
        semaphore = recv.at[len(groups)]
        groups.append(len(moves))
        return semaphore, begin_moves(semaphore, moves)

    def more(sent, moves):
        return sent[0], sent[1] + begin_moves(sent[0], moves)

    def arrived(sent):
        land(*sent)

    partner_of = {name: across(name) for name in "xyz"}
    place_of = {"x": x, "y": y, "z": z0}
    order_1 = (("yzx", 3), ("zyx", 3), ("xyz", 1), ("xzy", 1))
    order_c = (("yzx", 5), ("zyx", 5), ("xyz", 3), ("xzy", 3))
    order_2 = (("yzx", 5), ("zyx", 5), ("xyz", 3), ("xzy", 3))
    every = (slice(None),)

    def row_parts(count, orders):
        units = count // 8
        weight = sum(share for _, share in orders)
        result = []
        begin = seen = 0
        for order, share in orders:
            seen += share
            end = seen * units // weight * 8
            result.append((order, begin, end - begin))
            begin = end
        return result

    def tile(ref, lead, begin, size, far):
        where = tuple(1 - place_of[name] if name in far else place_of[name] for name in "zyx")
        return ref.at[lead + where + (core, pl.ds(begin, size))]

    def first_wave(ref, orders, lead=()):
        near_moves, last_moves = [], []
        parts = row_parts(ref.shape[-2], orders)
        for k in range(3):
            for order, begin, size in parts:
                box = tile(ref, lead, begin, size, "")
                move = (box, box, partner_of[order[k]])
                (last_moves if k == 2 else near_moves).append(move)
        started = ship(near_moves)
        last = ship(last_moves)
        return started, last

    def second_wave(ref, orders, sent, short, lead=()):
        near_moves, last_moves = [], []
        for order, begin, size in row_parts(ref.shape[-2], orders):
            p, q, r = order
            box = tile(ref, lead, begin, size, p)
            if short:
                near_moves.append((box, box, across(q + r)))
            near_moves.append((box, box, partner_of[q]))
            last_moves.append((box, box, partner_of[r]))
            box = tile(ref, lead, begin, size, q)
            last_moves.append((box, box, partner_of[r]))
        if short:
            return None, more(sent[1], near_moves + last_moves)
        started = ship(near_moves)
        return started, more(sent[1], last_moves)

    def third_wave(ref, orders, sent, lead=()):
        moves = []
        for order, begin, size in row_parts(ref.shape[-2], orders):
            box = tile(ref, lead, begin, size, order[:2])
            moves.append((box, box, partner_of[order[2]]))
        return more(sent[1], moves)

    def cross(ref, orders, fresh, lead=()):
        moves = []
        for order, begin, size in row_parts(ref.shape[-2], orders):
            where = []
            for name in "zyx":
                if name != order[2]:
                    where.append(slice(None))
                else:
                    where.append(1 - place_of[name] if fresh else place_of[name])
            box = ref.at[lead + tuple(where) + (core, pl.ds(begin, size))]
            moves.append((box, box, to_core))
        return ship(moves)

    def at(i):
        return slice(i * br, (i + 1) * br)

    def load_column(j):
        if j < 2:
            land(*got_blk[j])
        l_top[at(j), at(j)], l_low[at(j), at(j)] = halves(inv[j])
        for i in range(j + 1, nb):
            p = starts[j] + i - j - 1
            block = blk[p] * pat[0, p].astype(F32)
            l_top[at(i), at(j)], l_low[at(i), at(j)] = halves(block)

    pending = []
    forward = [None] * nb

    def begin_forward():
        pat_copy.wait()
        land(*got_main)
        pending.extend(rhs[at(i)] for i in range(nb))

    def forward_step(j):
        load_column(j)
        top, low = halves(pending[j])
        solved_j = wide(l_top[at(j), at(j)], l_low[at(j), at(j)], jnp.concatenate([top, low], 1))
        forward[j] = solved_j
        top, low = halves(solved_j)
        both = jnp.concatenate([top, low], 1)
        for i in range(j + 1, nb):
            pending[i] = pending[i] - wide(l_top[at(i), at(j)], l_low[at(i), at(j)], both)

    last_t = []

    def end_forward():
        land(*got_rest)
        e_top[...], e_low[...] = halves(cpl[...])
        last_t.append(forward[nb - 1].T)

    def make_part(l):
        pad[...] = jnp.zeros_like(pad)
        if l == 0:
            pad[pl.ds(pl.multiple_of((2 * z0 + y) * r1, r1), r1), :] = srhs[0:r1]
        else:
            pad[pl.ds(pl.multiple_of(leaf * r2, r2), r2), :] = srhs[r1 : r1 + r2]
        term = pad[...].T - tall(last_t[0], e_top[at(l), :], e_low[at(l), :])
        for h in range(2):
            part[l, h] = term[:, h * half : (h + 1) * half].reshape(2, 2, w, half)

    def send_part(l, short):
        if short:
            return ship([
                (part.at[l, :, 1 - z0, 1 - y], ra.at[l, 0], to_yz),
                (part.at[l, :, z0, 1 - y], ra.at[l, 1], to_y),
                (part.at[l, :, 1 - z0, y], ra.at[l, 2], to_z0),
            ])
        first = ship([(part.at[l, 0, 1 - z0, 1 - y], ra.at[l, 0, 0], to_y)])
        other = ship([(part.at[l, 1, 1 - z0, 1 - y], ra.at[l, 1, 0], to_z0)])
        last = ship([
            (part.at[l, 0, z0, 1 - y], ra.at[l, 0, 1], to_y),
            (part.at[l, 1, 1 - z0, y], ra.at[l, 1, 1], to_z0),
        ])
        return first, other, last

    def second(l, sent):
        arrived(sent[0])
        acc[l, 0] = part[l, 0, 1 - z0, y] + ra[l, 0, 0]
        last = more(sent[2], [(acc.at[l, 0], rb.at[l, 0], to_z0)])
        arrived(sent[1])
        acc[l, 1] = part[l, 1, z0, 1 - y] + ra[l, 1, 0]
        return more(last, [(acc.at[l, 1], rb.at[l, 1], to_y)])

    def total(l, sent, short):
        arrived(sent)
        if short:
            return jnp.concatenate(
                [part[l, h, z0, y] + ra[l, 0, h] + (ra[l, 1, h] + ra[l, 2, h]) for h in range(2)], 1
            )
        return jnp.concatenate([part[l, h, z0, y] + ra[l, h, 1] + rb[l, h] for h in range(2)], 1)

    row = lax.broadcasted_iota(jnp.int32, (br, br), 0)
    column = lax.broadcasted_iota(jnp.int32, (br, br), 1)
    unit = jnp.where(row == column, 1.0, 0.0).astype(F32)

    def backward_step(i):
        first = forward[i].T
        below = unit if i == nb - 1 else jnp.zeros((br, br), F32)
        target = jnp.concatenate([first, below], 0)
        if i < nb - 1:
            rest = slice((i + 1) * br, nb * br)
            target = target - (
                mm(xt_top[:, rest], l_top[rest, at(i)])
                + mm(xt_low[:, rest], l_top[rest, at(i)])
                + mm(xt_top[:, rest], l_low[rest, at(i)])
            )
        value = tall(target, l_top[at(i), at(i)], l_low[at(i), at(i)])
        xt_top[:, at(i)], xt_low[:, at(i)] = halves(value)
        solved[at(i), :] = value[:n].T
        top, low = halves(value[n:].T)
        lifted[at(i), 0:br] = top
        lifted[at(i), br : 2 * br] = low

    def spread(src, top_ref, low_ref, rows, lead):
        for k in range(lead):
            for c in range(4):
                if lead == 4:
                    tile = src[k // 2, k % 2, c // 2, c % 2]
                else:
                    tile = src[k // 4, k // 2 % 2, k % 2, c // 2, c % 2]
                where = (slice(k * rows, (k + 1) * rows), slice(c * tile.shape[1], (c + 1) * tile.shape[1]))
                top, low = halves(tile)
                top_ref[where] = top
                low_ref[where] = low

    def place(l, value):
        xg[l, 0, z0, y] = value[:, :half]
        xg[l, 1, z0, y] = value[:, half:]

    def give(l, value):
        place(l, value)
        box, other_box = xg.at[l, 0, z0, y], xg.at[l, 1, z0, y]
        first = ship([(box, box, to_y)])
        other = ship([(other_box, other_box, to_z0)])
        return first, other, ship([(box, box, to_z0), (other_box, other_box, to_y)])

    def give_more(l, sent):
        arrived(sent[0])
        box = xg.at[l, 0, z0, 1 - y]
        last = more(sent[2], [(box, box, to_z0)])
        arrived(sent[1])
        box = xg.at[l, 1, 1 - z0, y]
        return more(last, [(box, box, to_y)])

    def give_all(l, value):
        place(l, value)
        box = xg.at[l, :, z0, y]
        return ship([(box, box, target) for target in (to_yz, to_y, to_z0)])

    def against(top_ref, low_ref, l):
        result = None
        for h in range(2):
            top, low = halves(xg[l, h].reshape(n, half))
            lanes = slice(h * half, (h + 1) * half)
            both = mm(top_ref[:, lanes], jnp.concatenate([top, low], 0), NT)
            term = both[:, :n] + both[:, n:] + mm(low_ref[:, lanes], top, NT)
            result = term if result is None else result + term
        return result

    def make_u():
        tile = pl.ds(pl.multiple_of((2 * z0 + y) * r1, r1), r1)
        u_top[0:br, :], u_low[0:br, :] = halves(tall3(e_top[at(0), :], e_low[at(0), :], d1_top[...], d1_low[...], NT))
        u_top[br : 2 * br, :] = d1_top[:, tile].T
        u_low[br : 2 * br, :] = d1_low[:, tile].T

    def make_v():
        value = tall3(u_top[...], u_low[...], c_top[...], c_low[...], NN)
        v_top[0:br, :], v_low[0:br, :] = halves(cpl[at(1), :] - value[0:br])
        v_top[br : 2 * br, :], v_low[br : 2 * br, :] = halves(-value[br : 2 * br])

    def make_q():
        pair = pl.ds(pl.multiple_of((2 * z1 + z0) * 2 * r2, 2 * r2), 2 * r2)
        q_top[0 : 2 * br, :], q_low[0 : 2 * br, :] = halves(
            tall3(v_top[...], v_low[...], d2_top[...], d2_low[...], NT)
        )
        q_top[2 * br :, :] = d2_top[:, pair].T
        q_low[2 * br :, :] = d2_low[:, pair].T

    def make_r():
        r_top[...], r_low[...] = halves(tall3(q_top[...], q_low[...], d2_top[...], d2_low[...], NN))

    def rows_part(c):
        return pl.ds(c * (w // 2), w // 2)

    def give_part(l, c, sent):
        rows = rows_part(c)
        value = tsend[rows, :] + trecv[rows, :]
        xg[l, 0, z0, y, rows] = value[:, :half]
        xg[l, 1, z0, y, rows] = value[:, half:]
        box = xg.at[l, :, z0, y, rows]
        moves = [(box, box, target) for target in (to_yz, to_y, to_z0)]
        return ship(moves) if sent is None else more(sent, moves)

    begin_forward()
    land(*got_own)
    pl.semaphore_wait(barrier, len(partners))
    d1_s = first_wave(d1b, order_1)
    forward_step(0)
    forward_step(1)
    c_s = first_wave(cb, order_c)
    forward_step(2)
    forward_step(3)
    forward_step(4)
    d2_z = ship([(sinv.at[pl.ds(r1, r2)], d2b.at[z1, z0, y, x, core], to_z1)])
    arrived(d1_s[0])
    d1_s = second_wave(d1b, order_1, d1_s, False)
    forward_step(5)
    forward_step(6)
    end_forward()
    arrived(c_s[0])
    c_s = second_wave(cb, order_c, c_s, False)
    make_part(0)
    a1 = send_part(0, False)
    make_part(1)
    a2 = send_part(1, False)
    arrived(d1_s[0])
    d1_l = third_wave(d1b, order_1, d1_s)
    b1 = second(0, a1)
    arrived(c_s[0])
    c_l = third_wave(cb, order_c, c_s)
    backward_step(6)
    d1_d = cross(d1b, order_1, False)
    arrived(d2_z)
    d2_s = first_wave(d2b, order_2, lead=every)
    backward_step(5)
    c_d = cross(cb, order_c, False)
    backward_step(4)
    arrived(d1_l)
    d1_e = cross(d1b, order_1, True)
    arrived(d1_d)
    arrived(d1_e)
    spread(d1b, d1_top, d1_low, r1, 4)
    b2 = second(1, a2)
    arrived(c_l)
    c_e = cross(cb, order_c, True)
    arrived(d2_s[0])
    d2_s = second_wave(d2b, order_2, d2_s, False, lead=every)
    s_1 = total(0, b1, False)
    z_1 = tall(s_1, d1_top[...], d1_low[...], NT)
    make_u()
    arrived(c_d)
    arrived(c_e)
    spread(cb, c_top, c_low, r1, 4)
    g1 = give(0, z_1)
    s_2 = total(1, b2, False)
    tsend[...] = s_2 - tall(z_1, c_top[...], c_low[...])
    ts = [ship([(tsend.at[rows_part(c)], trecv.at[rows_part(c)], to_z1)]) for c in range(2)]
    arrived(d2_s[0])
    d2_l = third_wave(d2b, order_2, d2_s, lead=every)
    backward_step(3)
    make_v()
    g1 = give_more(0, g1)
    d2_d = cross(d2b, order_2, False, lead=every)
    backward_step(2)
    backward_step(1)
    arrived(ts[0])
    g2 = give_part(1, 0, None)
    arrived(d2_l)
    d2_e = cross(d2b, order_2, True, lead=every)
    arrived(ts[1])
    g2 = give_part(1, 1, g2)
    backward_step(0)
    arrived(d2_d)
    arrived(d2_e)
    spread(d2b, d2_top, d2_low, r2, 8)
    make_q()
    make_r()
    arrived(g1)
    base = against(u_top, u_low, 0)
    arrived(g2)
    rest = against(r_top, r_low, 1)
    top, low = halves(base[0:br] + rest[0:br])
    fixed[...] = jnp.concatenate([top, low], 1)
    sout[0:r1, :] = base[br : 2 * br] + rest[br : 2 * br]
    tmp[...] = rest[2 * br :]
    sout[r1 : r1 + r2, :] = tmp[pl.ds(pl.multiple_of(y * r2, r2), r2), :]
    land(send.at[0], sum(shipped))


def fused(leaf_rhs, leaf_inverse, leaf_blocks, leaf_pattern, leaf_coupling, sep_rhs, sep_inverse, sep_coupling):
    rows, n = leaf_rhs.shape
    br = leaf_inverse.shape[1]
    sep = leaf_coupling.shape[1]
    half, w = sep // 2, n // 4
    r1, r2 = sep // 4, sep // 8
    tile = sep_inverse.shape[1]
    vm = pl.BlockSpec(memory_space=pltpu.VMEM)
    V = pltpu.VMEM
    solved, lifted, fixed, sout = pl.pallas_call(
        whole_kernel,
        out_shape=(
            pltpu.VMEM((rows, n), F32),
            pltpu.VMEM((rows, 2 * br), BF16),
            pltpu.VMEM((br, 2 * n), BF16),
            pltpu.VMEM(sep_rhs.shape, F32),
        ),
        in_specs=[pl.BlockSpec(memory_space=pltpu.HBM)] * 8,
        out_specs=(vm, vm, vm, vm),
        scratch_shapes=[
            V(leaf_rhs.shape, F32), V(leaf_inverse.shape, F32), V(leaf_blocks.shape, F32),
            pltpu.SMEM(leaf_pattern.shape, jnp.int32),
            V(leaf_coupling.shape, F32), V(sep_rhs.shape, F32),
            V((rows, rows), BF16), V((rows, rows), BF16),
            V((n + br, rows), BF16), V((n + br, rows), BF16),
            V(leaf_coupling.shape, BF16), V(leaf_coupling.shape, BF16),
            V((2, 2, 2, 2, r1, tile), F32),
            V((2, 2, 2, 2, r1, tile), F32),
            V((2, 2, 2, 2, 2, r2, tile), F32),
            V((sep, sep), BF16), V((sep, sep), BF16),
            V((sep, sep), BF16), V((sep, sep), BF16),
            V((sep, sep), BF16), V((sep, sep), BF16),
            V((sep, n), F32),
            V((2, 2, 2, 2, w, half), F32),
            V((2, 3, 2, w, half), F32),
            V((2, 2, w, half), F32),
            V((2, 2, w, half), F32),
            V((w, sep), F32), V((w, sep), F32),
            V((2, 2, 2, 2, w, half), F32),
            V((2 * r2, n), F32),
            V((2 * br, sep), BF16), V((2 * br, sep), BF16),
            V((2 * br, sep), BF16), V((2 * br, sep), BF16),
            V((2 * br + 2 * r2, sep), BF16), V((2 * br + 2 * r2, sep), BF16),
            V((2 * br + 2 * r2, sep), BF16), V((2 * br + 2 * r2, sep), BF16),
            V((12 * 1024, 128), F32),
            pltpu.SemaphoreType.DMA((1,)),
            pltpu.SemaphoreType.DMA((28,)),
            pltpu.SemaphoreType.DMA((6,)),
        ],
        compiler_params=pltpu.CompilerParams(
            collective_id=0, has_side_effects=True, vmem_limit_bytes=65_800_000
        ),
    )(leaf_rhs, leaf_inverse, leaf_blocks, leaf_pattern, leaf_coupling, sep_rhs, sep_inverse, sep_coupling)

    return pl.pallas_call(
        finish_kernel,
        out_shape=(
            jax.ShapeDtypeStruct((rows, n), F32),
            jax.ShapeDtypeStruct(sep_rhs.shape, F32),
        ),
        in_specs=[vm] * 4,
        out_specs=[pl.BlockSpec(memory_space=pl.ANY)] * 2,
        scratch_shapes=[V((rows, n), F32), pltpu.SemaphoreType.DMA((2,))],
        compiler_params=pltpu.CompilerParams(vmem_limit_bytes=8 * 1024 * 1024),
    )(solved, lifted, fixed, sout)


def finish_kernel(solved, lifted, fixed, sout, out_far, sout_far, out, near):
    br = fixed.shape[0]
    sep_copy = pltpu.make_async_copy(sout, sout_far, near.at[0])
    sep_copy.start()
    both = fixed[...]
    for i in range(solved.shape[0] // br):
        rows = slice(i * br, (i + 1) * br)
        out[rows, :] = solved[rows, :] - wide(lifted[rows, 0:br], lifted[rows, br : 2 * br], both)
        pltpu.make_async_copy(out.at[pl.ds(i * br, br)], out_far.at[pl.ds(i * br, br)], near.at[1]).start()
    sep_copy.wait()
    pltpu.make_async_copy(out, out_far, near.at[1]).wait()


def pick(*args):
    leaf_rhs, leaf_inverse, _, _, leaf_coupling, _, sep_inverse, _ = args
    if (
        lax.axis_size("leaf") == 8
        and lax.axis_size("col") == 4
        and leaf_inverse.shape[1] == leaf_rhs.shape[1] == sep_inverse.shape[1]
        and leaf_coupling.shape[1] == 4 * sep_inverse.shape[1]
    ):
        return fused(*args)
    return shards(*args)


def solution(mesh):
    return jax.shard_map(
        pick,
        mesh=mesh,
        in_specs=(
            P("leaf", "col"),
            P("leaf", None, None),
            P("leaf", None, None),
            P("leaf", None),
            P("leaf", None),
            P("leaf", "col"),
            P("leaf", "col"),
            P("leaf", "col"),
        ),
        out_specs=(P("leaf", "col"), P("leaf", "col")),
        check_vma=False,
    )
```
